512 devices in a mesh: recv: 128 (over z, y_hi, x), tm: 4 (over y_lo, core).
Axes of the slice: x: 4, y: 8 (y_hi: 4, y_lo: 2; y = y_hi * 2 + y_lo), z: 8, core: 2. Of those that a mesh axis runs over, the one named last changes fastest.
Arguments:
- record: float32 [2048, 4096], P('recv', 'tm')
- source_channels: int32 [16], replicated, may hold values from 0 to 2047, as said below
- valid_mask: int32 [2048, 4], P('recv', 'tm'), may hold values 0 or 1
Outputs:
- lag_stack: float32 [16, 2048, 256], P('tm', 'recv')
The draws below stay inside these ranges and needn't reach their ends.
Inputs may be any that keep to these rules, and one draw needn't show every extreme that they name: `source_channels`: ascending and distinct; source s lies in channels s * 128 to (s + 1) * 128 - 1; the first is channel 0 and the last channel 2048 - 1.
All inputs are finite; a program needn't handle non-finite values. No bound on the sum of `valid_mask` on one device may be relied on, other than what follows from the above.
Results may differ from the reference program's by a relative error of at most 0.0001.
Values sent between devices are 32-bit elements; how exact they have to be, the bound alone decides.
A program may use at most 64 MiB of HBM per device.

```python
import jax
import jax.numpy as jnp
from jax import lax

SEGLEN = 2048
HOP = 1024
NF = 1024
LAGS = 256
SMOOTH = 64
NSRC = 16
R = 2048
SEGS = 4
NS = 4096


def draw_record(key, part):
    keys = jax.random.split(key, 6)
    white = jax.random.normal(keys[0], (R, NS), jnp.float32)
    common_weight = 0.7
    coef_one = jax.random.uniform(keys[1], (R, 1), jnp.float32, -0.8, 0.8)
    coef_two = jax.random.uniform(keys[2], (R, 1), jnp.float32, -0.6, 0.6)
    colored = white + coef_one * jnp.roll(white, 1, axis=1) + coef_two * jnp.roll(white, 2, axis=1)
    common = jax.random.normal(keys[3], (NS,), jnp.float32)
    delays = jax.random.randint(keys[4], (R, 1), 0, LAGS // 2)
    positions = (jnp.arange(NS)[None, :] - delays) % NS
    shifted = jnp.take(common, positions)
    levels = jnp.exp(jax.random.uniform(keys[5], (R, NS // HOP), jnp.float32, 0.0, 2.3))
    amplitude = jnp.repeat(levels, HOP, axis=1)
    return amplitude * (colored + common_weight * shifted)


def draw_source_channels(key, part):
    block_size = R // NSRC
    offsets = jax.random.randint(key, (NSRC,), 0, block_size)
    offsets = offsets.at[0].set(0).at[NSRC - 1].set(block_size - 1)
    return (jnp.arange(NSRC) * block_size + offsets).astype(jnp.int32)


def with_ends(values, rng, smallest, top_value):
    longest = values.shape.index(max(values.shape))
    spots = []
    for shift in (0, 1):
        where = [jax.random.randint(jax.random.fold_in(rng, axis), (), 0, length) for axis, length in enumerate(values.shape)]
        where[longest] = (where[longest] + shift) % values.shape[longest]
        spots.append(tuple(where))
    return values.at[spots[0]].set(smallest).at[spots[1]].set(top_value)


def setup_inputs(seed: int = 0) -> dict:
    splits = jax.random.split(jax.random.key(seed), 4)
    record = draw_record(jax.random.fold_in(splits[3], 71), 0)
    source_channels = draw_source_channels(jax.random.fold_in(splits[3], 71), 0)
    valid_mask = with_ends((jax.random.randint(splits[2], (R, SEGS), 0, 4) < 3).astype(jnp.int32), jax.random.fold_in(splits[2], 1), 0, 1)
    return {"record": record, "source_channels": source_channels, "valid_mask": valid_mask}


def reference(record, source_channels, valid_mask):
    chan_count = record.shape[0]
    padded = jnp.concatenate([record, jnp.zeros((chan_count, HOP), record.dtype)], axis=1)
    sample_idx = jnp.arange(SEGLEN)
    taper_weights = 0.5 - 0.5 * jnp.cos(2.0 * jnp.pi * sample_idx.astype(record.dtype) / SEGLEN)
    zero_init = jnp.zeros((), record.dtype)
    counts = lax.reduce_window(jnp.ones((1, NF), record.dtype), zero_init, lax.add, (1, 2 * SMOOTH + 1), (1, 1), [(0, 0), (SMOOTH, SMOOTH)])
    lag_index = (jnp.arange(LAGS) - LAGS // 2) % SEGLEN
    mask_float = valid_mask.astype(jnp.float32)

    def spectra_of(segment_no):
        segment = lax.dynamic_slice_in_dim(padded, segment_no * HOP, SEGLEN, 1)
        segment = (segment - lax.optimization_barrier(jnp.mean(segment, axis=1, keepdims=True))) * taper_weights
        spectrum = jnp.fft.rfft(segment, axis=1)[:, :NF]
        spec_re = jnp.real(spectrum)
        spec_im = jnp.imag(spectrum)
        power_spec = spec_re * spec_re + spec_im * spec_im
        smoothed = lax.reduce_window(power_spec, zero_init, lax.add, (1, 2 * SMOOTH + 1), (1, 1), [(0, 0), (SMOOTH, SMOOTH)]) / counts
        inv_scale = 1.0 / jnp.sqrt(smoothed + 1e-06)
        return (spec_re * inv_scale, spec_im * inv_scale)

    def add_segment(lag_stack, segment_no):
        white_re, white_im = spectra_of(segment_no)
        src_re = white_re[source_channels]
        src_im = white_im[source_channels]
        recv_valid = lax.dynamic_index_in_dim(mask_float, segment_no, 1, keepdims=False)
        src_valid = recv_valid[source_channels]

        def one_source(packed):
            one_re, one_im, one_valid = packed
            cross_re = one_re[None, :] * white_re + one_im[None, :] * white_im
            cross_im = one_re[None, :] * white_im - one_im[None, :] * white_re
            full = jnp.pad(lax.complex(cross_re, cross_im), ((0, 0), (0, 1)))
            lag_corr = jnp.take(jnp.fft.irfft(full, n=SEGLEN, axis=1), lag_index, axis=1)
            normed = lag_corr / jnp.sqrt(lax.optimization_barrier(jnp.mean(lag_corr * lag_corr, axis=1, keepdims=True)) + 1e-06)
            return normed * (one_valid * recv_valid)[:, None]
        return (lag_stack + lax.map(one_source, (src_re, src_im, src_valid)), None)
    start = jnp.zeros((NSRC, chan_count, LAGS), jnp.float32)
    lag_stack, unused = lax.scan(add_segment, start, jnp.arange(SEGS))
    return lag_stack
```

```python
import functools

import jax
import jax.numpy as jnp
import numpy as np
from jax import lax
from jax.experimental import pallas as pl
from jax.experimental.pallas import tpu as pltpu
from jax.sharding import PartitionSpec as P

SEGLEN = 2048
NF = 1024
LAGS = 256
SMOOTH = 64
NSRC = 16
SEGS = 4
ROWS = 16
HALF = 1024
LANES = 128
OWNERS = 8
PLANES = 8
COLS = 4
MINE = 4
MESH = pl.DeviceIdType.MESH


def split_bf16(table):
    bf16 = jnp.dtype(jnp.bfloat16)
    high = table.astype(bf16)
    low = (table - high.astype(np.float64)).astype(bf16)
    return high, low


@functools.cache
def tables():
    m = np.arange(16)[:, None]
    lane = np.arange(LANES)[None, :]
    taper = 0.5 - 0.5 * np.cos(2 * np.pi * (m * 128 + lane) / SEGLEN)
    twist = 2 * np.pi * m * lane / SEGLEN
    j = np.arange(8)[:, None]
    freq = j + 8 * (lane // 64) + 16 * (lane % 64)
    counts = np.minimum(freq + SMOOTH, NF - 1) - np.maximum(freq - SMOOTH, 0) + 1
    small = np.concatenate([taper, np.cos(twist), np.sin(twist), 1.0 / counts]).astype(np.float32)

    angle = 2 * np.pi * (np.arange(128)[:, None] * np.arange(64)[None, :] % 128) / 128
    forward = np.zeros((4, 128, 4, 64))
    for h in range(2):
        forward[2 * h, :, h] = np.cos(angle)
        forward[2 * h + 1, :, h] = np.sin(angle)
        forward[2 * h, :, 2 + h] = -np.sin(angle)
        forward[2 * h + 1, :, 2 + h] = np.cos(angle)
    forward = forward.reshape(512, 256)

    lag = np.arange(LAGS)[None, None, :] - LAGS // 2
    turn = 2 * np.pi * (freq[:, :, None] * lag % SEGLEN) / SEGLEN
    factor = np.where(freq == 0, 1.0, 2.0)[:, :, None] / SEGLEN
    inverse = np.stack([factor * np.cos(turn), -factor * np.sin(turn)], axis=1).reshape(2 * NF, LAGS)
    return small, np.stack(split_bf16(forward)), np.stack(split_bf16(inverse))


def halves(x):
    high = x.astype(jnp.bfloat16)
    low = (x - high.astype(jnp.float32)).astype(jnp.bfloat16)
    return high, low


def dot3(high, low, tab_high, tab_low):
    dot = functools.partial(jnp.dot, preferred_element_type=jnp.float32)
    return dot(high, tab_high) + dot(low, tab_high) + dot(high, tab_low)


def real_dft16(x):
    r2 = np.float32(np.sqrt(0.5))
    c1 = np.float32(np.cos(np.pi / 8))
    s1 = np.float32(np.sin(np.pi / 8))
    a = [x[m] + x[m + 8] for m in range(8)]
    b = [x[m] - x[m + 8] for m in range(8)]
    a2 = [a[m] + a[m + 4] for m in range(4)]
    b2 = [a[m] - a[m + 4] for m in range(4)]
    even, odd = a2[0] + a2[2], a2[1] + a2[3]
    out = [None] * 9
    out[0] = (even + odd, None)
    out[8] = (even - odd, None)
    out[4] = (a2[0] - a2[2], a2[3] - a2[1])
    diff, total = r2 * (b2[1] - b2[3]), r2 * (b2[1] + b2[3])
    out[2] = (b2[0] + diff, -(b2[2] + total))
    out[6] = (b2[0] - diff, b2[2] - total)
    u1, u2, u3 = b[1] - b[7], r2 * (b[2] - b[6]), b[3] - b[5]
    v1, v2, v3 = b[1] + b[7], r2 * (b[2] + b[6]), b[3] + b[5]
    up, um = b[0] + u2, b[0] - u2
    vp, vm = v2 + b[4], v2 - b[4]
    p, q = c1 * u1 + s1 * u3, s1 * u1 - c1 * u3
    out[1] = (up + p, -(s1 * v1 + c1 * v3 + vp))
    out[7] = (up - p, -(s1 * v1 + c1 * v3 - vp))
    out[3] = (um + q, -(c1 * v1 - s1 * v3 + vm))
    out[5] = (um - q, -(c1 * v1 - s1 * v3 - vm))
    return out


def whitened(x, small, forward):
    total = x[0]
    for m in range(1, 16):
        total = total + x[m]
    mean = jnp.sum(total, axis=1, keepdims=True) * (1.0 / SEGLEN)
    tapered = [(x[m] - mean) * small[m : m + 1, :] for m in range(16)]
    base = real_dft16(tapered)
    mid = []
    for f in range(16):
        re, im = base[min(f, 16 - f)]
        if im is not None and f > 8:
            im = -im
        cos, sin = small[16 + f : 17 + f, :], small[32 + f : 33 + f, :]
        if f == 0:
            mid.append((re, jnp.zeros_like(re)))
        elif im is None:
            mid.append((re * cos, -(re * sin)))
        else:
            mid.append((re * cos + im * sin, im * cos - re * sin))
    highs, lows = [], []
    for j in range(8):
        parts = [halves(v) for v in (*mid[j], *mid[j + 8])]
        highs.append(jnp.concatenate([p[0] for p in parts], axis=1))
        lows.append(jnp.concatenate([p[1] for p in parts], axis=1))
    spec = dot3(jnp.concatenate(highs, axis=0), jnp.concatenate(lows, axis=0), forward[0], forward[1])
    rows = x[0].shape[0]
    re = [spec[j * rows : (j + 1) * rows, :LANES] for j in range(8)]
    im = [spec[j * rows : (j + 1) * rows, LANES:] for j in range(8)]
    power = [re[j] * re[j] + im[j] * im[j] for j in range(8)]

    lane = lax.broadcasted_iota(jnp.int32, power[0].shape, 1)
    bin_g = lane % 64
    lower = lane < 64
    zero = jnp.zeros_like(power[0])
    ahead, behind = [power[0]], [power[7]]
    for j in range(1, 8):
        ahead.append(ahead[-1] + power[j])
        behind.append(behind[-1] + power[7 - j])
    behind.reverse()
    other = pltpu.roll(ahead[7], 64, 1)
    lower_total = jnp.where(lower, zero, other)
    upper_total = jnp.where(lower, other, zero)
    all_f = jnp.where(lower, ahead[7] + other, zero)
    three = all_f + pltpu.roll(all_f, 1, 1) + pltpu.roll(all_f, 2, 1)
    seven = jnp.where(lower, pltpu.roll(three, 125, 1) + all_f + pltpu.roll(three, 1, 1), zero)
    seven = seven + pltpu.roll(seven, 64, 1)
    out_re, out_im = [], []
    for j in range(8):
        above = jnp.where(bin_g < 60, pltpu.roll(ahead[j] + lower_total, 124, 1), zero)
        below = jnp.where(bin_g >= 4, pltpu.roll(behind[j] + upper_total, 4, 1), zero)
        smoothed = (seven + above + below) * small[48 + j : 49 + j, :]
        scale = lax.rsqrt(smoothed + 1e-06)
        out_re.append(re[j] * scale)
        out_im.append(im[j] * scale)
    return out_re, out_im


def kernel(
    chan_ref, mask_ref, rec_ref, small_ref, fwd_hbm, inv_hbm, out_ref,
    fwd_ref, inv_ref, all_ref, val_ref, vsend_ref, send1_ref, recv1_ref, send2_ref, recv2_ref,
    white_ref, src_ref, high_ref, low_ref,
    tab_sem, rec_ssem, rec_rsem, val_ssem, val_rsem, ssem1, rsem1, ssem2, rsem2,
):
    r = lax.axis_index("recv")
    t = lax.axis_index("tm")
    x, yh, z = r % COLS, (r // COLS) % 4, r // 16
    cand = r % OWNERS
    group = r // OWNERS
    dest = z // 2

    load_fwd = pltpu.make_async_copy(fwd_hbm, fwd_ref, tab_sem.at[0])
    load_inv = pltpu.make_async_copy(inv_hbm, inv_ref, tab_sem.at[1])
    load_fwd.start()
    load_inv.start()

    barrier = pltpu.get_barrier_semaphore()

    def greet(recv, tm):
        pl.semaphore_signal(barrier, inc=1, device_id={"recv": recv, "tm": tm}, device_id_type=MESH)

    for d in range(1, OWNERS):
        greet(group * OWNERS + (cand + d) % OWNERS, t)
    for d in range(1, SEGS):
        greet(r, (t + d) % SEGS)
    for p in range(2):
        for b in range(SEGS):
            for flip in range(2):
                plane = 2 * t + p
                row = yh if flip == 0 else 3 - yh
                if flip == 0:

                    @pl.when(jnp.logical_or(plane != z, t != b))
                    def _(plane=plane, row=row, b=b):
                        greet(plane * 16 + row * COLS + x, b)
                else:
                    greet(plane * 16 + row * COLS + x, b)

    rec = rec_ref[...]
    valid = jnp.broadcast_to(mask_ref[...].astype(jnp.float32), (ROWS, LANES))
    vsend_ref[...] = valid
    val_ref[t] = valid
    all_ref[t] = rec
    all_ref[SEGS] = jnp.zeros((ROWS, HALF), jnp.float32)

    index = jnp.clip(chan_ref[group] - r * ROWS, 0, ROWS - 1)
    picked = rec_ref[pl.ds(index, 1), :]
    for m in range(8):
        piece = picked[:, m * LANES : (m + 1) * LANES]
        send1_ref[pl.ds(m, 1), :] = piece
        recv1_ref[cand, pl.ds(m, 1), :] = piece
    piece = vsend_ref[pl.ds(index, 1), :]
    send1_ref[pl.ds(8, 1), :] = piece
    recv1_ref[cand, pl.ds(8, 1), :] = piece

    is_self = (t == dest).astype(jnp.int32)
    pl.semaphore_wait(barrier, (OWNERS - 1) + (SEGS - 1) + 16 - is_self)

    sends = []
    for d in range(1, OWNERS):
        copy = pltpu.make_async_remote_copy(
            send1_ref, recv1_ref.at[cand], ssem1.at[d], rsem1.at[cand],
            device_id={"recv": group * OWNERS + (cand + d) % OWNERS, "tm": t}, device_id_type=MESH,
        )
        copy.start()
        sends.append(copy)
    for d in range(1, SEGS):
        to = {"recv": r, "tm": (t + d) % SEGS}
        copy = pltpu.make_async_remote_copy(
            rec_ref, all_ref.at[t], rec_ssem.at[d], rec_rsem.at[t], device_id=to, device_id_type=MESH
        )
        copy.start()
        sends.append(copy)
        copy = pltpu.make_async_remote_copy(
            vsend_ref, val_ref.at[t], val_ssem.at[d], val_rsem.at[t], device_id=to, device_id_type=MESH
        )
        copy.start()
        sends.append(copy)

    def arrived(buf, sem):
        pltpu.make_async_remote_copy(
            buf, buf, sem, sem, device_id={"recv": r, "tm": t}, device_id_type=MESH
        ).wait_recv()

    for d in range(1, OWNERS):
        slot = (cand + d) % OWNERS
        arrived(recv1_ref.at[slot], rsem1.at[slot])

    owner = jnp.clip((chan_ref[group] - group * (OWNERS * ROWS)) // ROWS, 0, OWNERS - 1)
    chosen = recv1_ref[owner]
    send2_ref[...] = chosen
    entry = t * MINE + (z % 2) * 2 + yh // 2

    @pl.when(t == dest)
    def _():
        recv2_ref[entry] = chosen

    sends2 = []
    for n, dz in enumerate((4, 3, 5, 2, 6, 1, 7, 0)):
        for flip in range(2):
            row = yh if flip == 0 else 3 - yh
            copy = pltpu.make_async_remote_copy(
                send2_ref, recv2_ref.at[entry], ssem2.at[2 * n + flip], rsem2.at[entry],
                device_id={"recv": ((z + dz) % PLANES) * 16 + row * COLS + x, "tm": dest},
                device_id_type=MESH,
            )
            if dz == 0 and flip == 0:
                pl.when(t != dest)(copy.start)
            else:
                copy.start()
                sends.append(copy)
            sends2.append(copy)

    for d in range(1, SEGS):
        slot = (t + d) % SEGS
        arrived(all_ref.at[slot], rec_rsem.at[slot])
        arrived(val_ref.at[slot], val_rsem.at[slot])
    load_fwd.wait()
    small = small_ref[...]

    @pl.loop(0, SEGS)
    def _(k):
        first, second = all_ref[k], all_ref[k + 1]
        xs = [first[:, m * LANES : (m + 1) * LANES] for m in range(8)]
        xs += [second[:, m * LANES : (m + 1) * LANES] for m in range(8)]
        re, im = whitened(xs, small, (fwd_ref[0], fwd_ref[1]))
        for j in range(8):
            white_ref[k, j, :, :LANES] = re[j]
            white_ref[k, j, :, LANES:] = im[j]

    for e in range(SEGS * MINE):
        b, p, h = e // MINE, (e % MINE) // 2, e % 2
        own = jnp.logical_and(jnp.logical_and(t == b, z == 2 * t + p), yh // 2 == h)

        @pl.when(jnp.logical_not(own))
        def _(e=e):
            arrived(recv2_ref.at[e], rsem2.at[e])

    none = jnp.zeros((MINE, LANES), jnp.float32)
    xs = [recv2_ref[:, m, :] for m in range(8)]
    xs += [jnp.concatenate([v[MINE:], none], axis=0) for v in xs]
    re, im = whitened(xs, small, (fwd_ref[0], fwd_ref[1]))
    for j in range(8):
        src_ref[j, :, :LANES] = re[j]
        src_ref[j, :, LANES:] = im[j]

    @pl.loop(0, SEGS)
    def _(k):
        for j in range(8):
            rec_re, rec_im = white_ref[k, j, :, :LANES], white_ref[k, j, :, LANES:]
            for s in range(MINE):
                src = src_ref[j, pl.ds(k * MINE + s, 1), :]
                src_re, src_im = src[:, :LANES], src[:, LANES:]
                cross_re = src_re * rec_re + src_im * rec_im
                cross_im = src_re * rec_im - src_im * rec_re
                rows = pl.ds(pl.multiple_of(k * (MINE * ROWS), MINE * ROWS) + s * ROWS, ROWS)
                for part, value in enumerate((cross_re, cross_im)):
                    high, low = halves(value)
                    first = (2 * j + part) * LANES
                    high_ref[rows, first : first + LANES] = high
                    low_ref[rows, first : first + LANES] = low

    load_inv.wait()
    lag = dot3(high_ref[...], low_ref[...], inv_ref[0], inv_ref[1])
    power = jnp.sum(lag * lag, axis=1, keepdims=True) * (1.0 / LAGS)
    scale = lax.rsqrt(power + 1e-06)
    for s in range(MINE):
        stack = None
        for k in range(SEGS):
            first = (k * MINE + s) * ROWS
            weight = val_ref[k] * recv2_ref[k * MINE + s, pl.ds(8, 1), :]
            term = lag[first : first + ROWS] * (scale[first : first + ROWS] * weight[:, :1])
            stack = term if stack is None else stack + term
        out_ref[s] = stack

    for copy in sends:
        copy.wait_send()

    @pl.when(t != dest)
    def _():
        sends2[14].wait_send()


def local(record, source_channels, valid_mask):
    small, forward, inverse = tables()
    f32, bf16 = jnp.float32, jnp.bfloat16
    vmem = pl.BlockSpec(memory_space=pltpu.VMEM)
    hbm = pl.BlockSpec(memory_space=pltpu.HBM)
    dma = pltpu.SemaphoreType.DMA
    return pl.pallas_call(
        kernel,
        out_shape=jax.ShapeDtypeStruct((MINE, ROWS, LAGS), f32),
        in_specs=[pl.BlockSpec(memory_space=pltpu.SMEM), vmem, vmem, vmem, hbm, hbm],
        out_specs=vmem,
        scratch_shapes=[
            pltpu.VMEM((2, 512, 256), bf16),
            pltpu.VMEM((2, 2 * NF, LAGS), bf16),
            pltpu.VMEM((SEGS + 1, ROWS, HALF), f32),
            pltpu.VMEM((SEGS, ROWS, LANES), f32),
            pltpu.VMEM((ROWS, LANES), f32),
            pltpu.VMEM((9, LANES), f32),
            pltpu.VMEM((OWNERS, 9, LANES), f32),
            pltpu.VMEM((9, LANES), f32),
            pltpu.VMEM((SEGS * MINE, 9, LANES), f32),
            pltpu.VMEM((SEGS, 8, ROWS, 256), f32),
            pltpu.VMEM((8, SEGS * MINE, 256), f32),
            pltpu.VMEM((SEGS * MINE * ROWS, 2 * NF), bf16),
            pltpu.VMEM((SEGS * MINE * ROWS, 2 * NF), bf16),
            dma((2,)), dma((SEGS,)), dma((SEGS,)), dma((SEGS,)), dma((SEGS,)),
            dma((OWNERS,)), dma((OWNERS,)), dma((16,)), dma((16,)),
        ],
        compiler_params=pltpu.CompilerParams(
            collective_id=0, has_side_effects=True, vmem_limit_bytes=60 * 2**20
        ),
        name="correlate",
    )(source_channels, valid_mask, record, jnp.asarray(small), jnp.asarray(forward), jnp.asarray(inverse))


def solution(mesh):
    placed = (P("recv", "tm"), P(), P("recv", "tm"))
    return jax.shard_map(
        local, mesh=mesh, in_specs=placed, out_specs=P("tm", "recv", None), check_vma=False
    )
```

```python
import functools

import jax
import jax.numpy as jnp
import numpy as np
from jax import lax
from jax.experimental import pallas as pl
from jax.experimental.pallas import tpu as pltpu
from jax.sharding import PartitionSpec as P

SEGLEN = 2048
NF = 1024
LAGS = 256
SMOOTH = 64
NSRC = 16
SEGS = 4
ROWS = 16
HALF = 1024
LANES = 128
OWNERS = 8
PLANES = 8
COLS = 4
MINE = 4
MESH = pl.DeviceIdType.MESH


def split_bf16(table):
    bf16 = jnp.dtype(jnp.bfloat16)
    high = table.astype(bf16)
    low = (table - high.astype(np.float64)).astype(bf16)
    return high, low


@functools.cache
def tables():
    m = np.arange(16)[:, None]
    lane = np.arange(LANES)[None, :]
    taper = 0.5 - 0.5 * np.cos(2 * np.pi * (m * 128 + lane) / SEGLEN)
    twist = 2 * np.pi * m * lane / SEGLEN
    j = np.arange(8)[:, None]
    freq = j + 8 * (lane // 64) + 16 * (lane % 64)
    counts = np.minimum(freq + SMOOTH, NF - 1) - np.maximum(freq - SMOOTH, 0) + 1
    small = np.concatenate([taper, np.cos(twist), np.sin(twist), 1.0 / counts]).astype(np.float32)

    angle = 2 * np.pi * (np.arange(128)[:, None] * np.arange(64)[None, :] % 128) / 128
    forward = np.zeros((4, 128, 4, 64))
    for h in range(2):
        forward[2 * h, :, h] = np.cos(angle)
        forward[2 * h + 1, :, h] = np.sin(angle)
        forward[2 * h, :, 2 + h] = -np.sin(angle)
        forward[2 * h + 1, :, 2 + h] = np.cos(angle)
    forward = forward.reshape(512, 256)

    lag = np.arange(LAGS)[None, None, :] - LAGS // 2
    turn = 2 * np.pi * (freq[:, :, None] * lag % SEGLEN) / SEGLEN
    factor = np.where(freq == 0, 1.0, 2.0)[:, :, None] / SEGLEN
    inverse = np.stack([factor * np.cos(turn), -factor * np.sin(turn)], axis=1).reshape(2 * NF, LAGS)
    return small, np.stack(split_bf16(forward)), np.stack(split_bf16(inverse))


def halves(x):
    high = x.astype(jnp.bfloat16)
    low = (x - high.astype(jnp.float32)).astype(jnp.bfloat16)
    return high, low


def dot3(high, low, tab_high, tab_low):
    dot = functools.partial(jnp.dot, preferred_element_type=jnp.float32)
    return dot(high, tab_high) + dot(low, tab_high) + dot(high, tab_low)


def real_dft16(x):
    r2 = np.float32(np.sqrt(0.5))
    c1 = np.float32(np.cos(np.pi / 8))
    s1 = np.float32(np.sin(np.pi / 8))
    a = [x[m] + x[m + 8] for m in range(8)]
    b = [x[m] - x[m + 8] for m in range(8)]
    a2 = [a[m] + a[m + 4] for m in range(4)]
    b2 = [a[m] - a[m + 4] for m in range(4)]
    even, odd = a2[0] + a2[2], a2[1] + a2[3]
    out = [None] * 9
    out[0] = (even + odd, None)
    out[8] = (even - odd, None)
    out[4] = (a2[0] - a2[2], a2[3] - a2[1])
    diff, total = r2 * (b2[1] - b2[3]), r2 * (b2[1] + b2[3])
    out[2] = (b2[0] + diff, -(b2[2] + total))
    out[6] = (b2[0] - diff, b2[2] - total)
    u1, u2, u3 = b[1] - b[7], r2 * (b[2] - b[6]), b[3] - b[5]
    v1, v2, v3 = b[1] + b[7], r2 * (b[2] + b[6]), b[3] + b[5]
    up, um = b[0] + u2, b[0] - u2
    vp, vm = v2 + b[4], v2 - b[4]
    p, q = c1 * u1 + s1 * u3, s1 * u1 - c1 * u3
    out[1] = (up + p, -(s1 * v1 + c1 * v3 + vp))
    out[7] = (up - p, -(s1 * v1 + c1 * v3 - vp))
    out[3] = (um + q, -(c1 * v1 - s1 * v3 + vm))
    out[5] = (um - q, -(c1 * v1 - s1 * v3 - vm))
    return out


def whitened(x, small, forward):
    total = x[0]
    for m in range(1, 16):
        total = total + x[m]
    mean = jnp.sum(total, axis=1, keepdims=True) * (1.0 / SEGLEN)
    tapered = [(x[m] - mean) * small[m : m + 1, :] for m in range(16)]
    base = real_dft16(tapered)
    mid = []
    for f in range(16):
        re, im = base[min(f, 16 - f)]
        if im is not None and f > 8:
            im = -im
        cos, sin = small[16 + f : 17 + f, :], small[32 + f : 33 + f, :]
        if f == 0:
            mid.append((re, jnp.zeros_like(re)))
        elif im is None:
            mid.append((re * cos, -(re * sin)))
        else:
            mid.append((re * cos + im * sin, im * cos - re * sin))
    highs, lows = [], []
    for j in range(8):
        parts = [halves(v) for v in (*mid[j], *mid[j + 8])]
        highs.append(jnp.concatenate([p[0] for p in parts], axis=1))
        lows.append(jnp.concatenate([p[1] for p in parts], axis=1))
    spec = dot3(jnp.concatenate(highs, axis=0), jnp.concatenate(lows, axis=0), forward[0], forward[1])
    rows = x[0].shape[0]
    re = [spec[j * rows : (j + 1) * rows, :LANES] for j in range(8)]
    im = [spec[j * rows : (j + 1) * rows, LANES:] for j in range(8)]
    power = [re[j] * re[j] + im[j] * im[j] for j in range(8)]

    lane = lax.broadcasted_iota(jnp.int32, power[0].shape, 1)
    bin_g = lane % 64
    lower = lane < 64
    zero = jnp.zeros_like(power[0])
    ahead, behind = [power[0]], [power[7]]
    for j in range(1, 8):
        ahead.append(ahead[-1] + power[j])
        behind.append(behind[-1] + power[7 - j])
    behind.reverse()
    other = pltpu.roll(ahead[7], 64, 1)
    lower_total = jnp.where(lower, zero, other)
    upper_total = jnp.where(lower, other, zero)
    all_f = jnp.where(lower, ahead[7] + other, zero)
    three = all_f + pltpu.roll(all_f, 1, 1) + pltpu.roll(all_f, 2, 1)
    seven = jnp.where(lower, pltpu.roll(three, 125, 1) + all_f + pltpu.roll(three, 1, 1), zero)
    seven = seven + pltpu.roll(seven, 64, 1)
    out_re, out_im = [], []
    for j in range(8):
        above = jnp.where(bin_g < 60, pltpu.roll(ahead[j] + lower_total, 124, 1), zero)
        below = jnp.where(bin_g >= 4, pltpu.roll(behind[j] + upper_total, 4, 1), zero)
        smoothed = (seven + above + below) * small[48 + j : 49 + j, :]
        scale = lax.rsqrt(smoothed + 1e-06)
        out_re.append(re[j] * scale)
        out_im.append(im[j] * scale)
    return out_re, out_im


def kernel(
    chan_ref, mask_ref, rec_ref, small_ref, fwd_hbm, inv_hbm, out_ref,
    fwd_ref, inv_ref, all_ref, val_ref, vsend_ref, send1_ref, recv1_ref, send2_ref, recv2_ref,
    white_ref, src_ref, high_ref, low_ref,
    tab_sem, rec_ssem, rec_rsem, val_ssem, val_rsem, ssem1, rsem1, ssem2, rsem2, ready_sem,
):
    r = lax.axis_index("recv")
    t = lax.axis_index("tm")
    x, yh, z = r % COLS, (r // COLS) % 4, r // 16
    cand = r % OWNERS
    group = r // OWNERS
    dest = z // 2

    load_fwd = pltpu.make_async_copy(fwd_hbm, fwd_ref, tab_sem.at[0])
    load_inv = pltpu.make_async_copy(inv_hbm, inv_ref, tab_sem.at[1])
    load_fwd.start()
    load_inv.start()

    barrier = pltpu.get_barrier_semaphore()

    def greet(recv, tm):
        pl.semaphore_signal(barrier, inc=1, device_id={"recv": recv, "tm": tm}, device_id_type=MESH)

    rows = (yh, 3 - yh)
    for d in range(1, OWNERS):
        greet(group * OWNERS + (cand + d) % OWNERS, t)
    for d in range(1, SEGS):
        greet(r, (t + d) % SEGS)

    @pl.when(t == dest)
    def _():
        for b in range(SEGS):
            greet(z * 16 + rows[1] * COLS + x, b)

    for p in range(2):

        @pl.when(2 * t + p > z)
        def _(p=p):
            for b in range(SEGS):
                for row in rows:
                    greet((2 * t + p) * 16 + row * COLS + x, b)

    for target in range(1, PLANES):

        @pl.when(target > z)
        def _(target=target):
            for row in rows:
                greet(target * 16 + row * COLS + x, dest)

    rec = rec_ref[...]
    mask = jnp.broadcast_to(mask_ref[...].astype(jnp.float32), (ROWS, ROWS))
    square = (ROWS, ROWS)
    diagonal = lax.broadcasted_iota(jnp.int32, square, 0) == lax.broadcasted_iota(jnp.int32, square, 1)
    mask = jnp.sum(jnp.where(diagonal, mask, 0.0), axis=1, keepdims=True)
    valid = jnp.broadcast_to(mask, (ROWS, LANES))
    vsend_ref[...] = valid
    val_ref[t] = valid
    all_ref[t] = rec
    all_ref[SEGS] = jnp.zeros((ROWS, HALF), jnp.float32)

    index = jnp.clip(chan_ref[group] - r * ROWS, 0, ROWS - 1)
    picked = rec_ref[pl.ds(index, 1), :]
    for m in range(8):
        piece = picked[:, m * LANES : (m + 1) * LANES]
        send1_ref[pl.ds(m, 1), :] = piece
        recv1_ref[cand, pl.ds(m, 1), :] = piece
    piece = vsend_ref[pl.ds(index, 1), :]
    send1_ref[pl.ds(8, 1), :] = piece
    recv1_ref[cand, pl.ds(8, 1), :] = piece

    lower_holders = jnp.clip(z - 2 * t, 0, 2)
    pl.semaphore_wait(barrier, (OWNERS - 1) + (SEGS - 1) + 1 + 2 * z + 8 * lower_holders)

    for p in range(2):

        @pl.when(2 * t + p < z)
        def _(p=p):
            for b in range(SEGS):
                for flip, row in enumerate(rows):
                    pl.semaphore_signal(
                        ready_sem.at[2 * z + flip], inc=1,
                        device_id={"recv": (2 * t + p) * 16 + row * COLS + x, "tm": b}, device_id_type=MESH,
                    )

    sends = []
    for d in range(1, OWNERS):
        copy = pltpu.make_async_remote_copy(
            send1_ref, recv1_ref.at[cand], ssem1.at[d], rsem1.at[cand],
            device_id={"recv": group * OWNERS + (cand + d) % OWNERS, "tm": t}, device_id_type=MESH,
        )
        copy.start()
        sends.append(copy)
    for d in range(1, SEGS):
        to = {"recv": r, "tm": (t + d) % SEGS}
        copy = pltpu.make_async_remote_copy(
            rec_ref, all_ref.at[t], rec_ssem.at[d], rec_rsem.at[t], device_id=to, device_id_type=MESH
        )
        copy.start()
        sends.append(copy)
        copy = pltpu.make_async_remote_copy(
            vsend_ref, val_ref.at[t], val_ssem.at[d], val_rsem.at[t], device_id=to, device_id_type=MESH
        )
        copy.start()
        sends.append(copy)

    def arrived(buf, sem):
        pltpu.make_async_remote_copy(
            buf, buf, sem, sem, device_id={"recv": r, "tm": t}, device_id_type=MESH
        ).wait_recv()

    for d in range(1, OWNERS):
        slot = (cand + d) % OWNERS
        arrived(recv1_ref.at[slot], rsem1.at[slot])

    owner = jnp.clip((chan_ref[group] - group * (OWNERS * ROWS)) // ROWS, 0, OWNERS - 1)
    chosen = recv1_ref[owner]
    send2_ref[...] = chosen
    entry = t * MINE + (z % 2) * 2 + yh // 2

    @pl.when(t == dest)
    def _():
        recv2_ref[entry] = chosen

    def spread(target, flip):
        return pltpu.make_async_remote_copy(
            send2_ref, recv2_ref.at[entry], ssem2.at[2 * target + flip], rsem2.at[entry],
            device_id={"recv": target * 16 + rows[flip] * COLS + x, "tm": dest}, device_id_type=MESH,
        )

    for target in range(PLANES):
        pl.when(target <= z)(spread(target, 1).start)
        pl.when(jnp.logical_or(target < z, jnp.logical_and(target == z, t != dest)))(spread(target, 0).start)

    for d in range(1, SEGS):
        slot = (t + d) % SEGS
        arrived(all_ref.at[slot], rec_rsem.at[slot])
        arrived(val_ref.at[slot], val_rsem.at[slot])
    load_fwd.wait()
    small = small_ref[...]

    @pl.loop(0, SEGS)
    def _(k):
        first, second = all_ref[k], all_ref[k + 1]
        xs = [first[:, m * LANES : (m + 1) * LANES] for m in range(8)]
        xs += [second[:, m * LANES : (m + 1) * LANES] for m in range(8)]
        re, im = whitened(xs, small, (fwd_ref[0], fwd_ref[1]))
        for j in range(8):
            white_ref[k, j, :, :LANES] = re[j]
            white_ref[k, j, :, LANES:] = im[j]

    for target in range(1, PLANES):

        @pl.when(target > z)
        def _(target=target):
            for flip in range(2):
                pl.semaphore_wait(ready_sem.at[2 * target + flip], 1)
                spread(target, flip).start()

    for e in range(SEGS * MINE):
        b, p, h = e // MINE, (e % MINE) // 2, e % 2
        own = jnp.logical_and(jnp.logical_and(t == b, z == 2 * t + p), yh // 2 == h)

        @pl.when(jnp.logical_not(own))
        def _(e=e):
            arrived(recv2_ref.at[e], rsem2.at[e])

    none = jnp.zeros((MINE, LANES), jnp.float32)
    xs = [recv2_ref[:, m, :] for m in range(8)]
    xs += [jnp.concatenate([v[MINE:], none], axis=0) for v in xs]
    re, im = whitened(xs, small, (fwd_ref[0], fwd_ref[1]))
    for j in range(8):
        src_ref[j, :, :LANES] = re[j]
        src_ref[j, :, LANES:] = im[j]

    @pl.loop(0, SEGS)
    def _(k):
        for j in range(8):
            rec_re, rec_im = white_ref[k, j, :, :LANES], white_ref[k, j, :, LANES:]
            for s in range(MINE):
                src = src_ref[j, pl.ds(k * MINE + s, 1), :]
                src_re, src_im = src[:, :LANES], src[:, LANES:]
                cross_re = src_re * rec_re + src_im * rec_im
                cross_im = src_re * rec_im - src_im * rec_re
                rows = pl.ds(pl.multiple_of(k * (MINE * ROWS), MINE * ROWS) + s * ROWS, ROWS)
                for part, value in enumerate((cross_re, cross_im)):
                    high, low = halves(value)
                    first = (2 * j + part) * LANES
                    high_ref[rows, first : first + LANES] = high
                    low_ref[rows, first : first + LANES] = low

    load_inv.wait()
    lag = dot3(high_ref[...], low_ref[...], inv_ref[0], inv_ref[1])
    power = jnp.sum(lag * lag, axis=1, keepdims=True) * (1.0 / LAGS)
    scale = lax.rsqrt(power + 1e-06)
    for s in range(MINE):
        stack = None
        for k in range(SEGS):
            first = (k * MINE + s) * ROWS
            weight = val_ref[k] * recv2_ref[k * MINE + s, pl.ds(8, 1), :]
            term = lag[first : first + ROWS] * (scale[first : first + ROWS] * weight[:, :1])
            stack = term if stack is None else stack + term
        out_ref[s] = stack

    for copy in sends:
        copy.wait_send()

    for target in range(PLANES):
        spread(target, 1).wait_send()
        pl.when(jnp.logical_or(target != z, t != dest))(spread(target, 0).wait_send)


def local(record, source_channels, valid_mask):
    small, forward, inverse = tables()
    f32, bf16 = jnp.float32, jnp.bfloat16
    vmem = pl.BlockSpec(memory_space=pltpu.VMEM)
    hbm = pl.BlockSpec(memory_space=pltpu.HBM)
    dma = pltpu.SemaphoreType.DMA
    return pl.pallas_call(
        kernel,
        out_shape=jax.ShapeDtypeStruct((MINE, ROWS, LAGS), f32),
        in_specs=[pl.BlockSpec(memory_space=pltpu.SMEM), vmem, vmem, vmem, hbm, hbm],
        out_specs=vmem,
        scratch_shapes=[
            pltpu.VMEM((2, 512, 256), bf16),
            pltpu.VMEM((2, 2 * NF, LAGS), bf16),
            pltpu.VMEM((SEGS + 1, ROWS, HALF), f32),
            pltpu.VMEM((SEGS, ROWS, LANES), f32),
            pltpu.VMEM((ROWS, LANES), f32),
            pltpu.VMEM((9, LANES), f32),
            pltpu.VMEM((OWNERS, 9, LANES), f32),
            pltpu.VMEM((9, LANES), f32),
            pltpu.VMEM((SEGS * MINE, 9, LANES), f32),
            pltpu.VMEM((SEGS, 8, ROWS, 256), f32),
            pltpu.VMEM((8, SEGS * MINE, 256), f32),
            pltpu.VMEM((SEGS * MINE * ROWS, 2 * NF), bf16),
            pltpu.VMEM((SEGS * MINE * ROWS, 2 * NF), bf16),
            dma((2,)), dma((SEGS,)), dma((SEGS,)), dma((SEGS,)), dma((SEGS,)),
            dma((OWNERS,)), dma((OWNERS,)), dma((16,)), dma((16,)), pltpu.SemaphoreType.REGULAR((16,)),
        ],
        compiler_params=pltpu.CompilerParams(
            collective_id=0, has_side_effects=True, vmem_limit_bytes=60 * 2**20
        ),
        name="correlate",
    )(source_channels, valid_mask.reshape(1, ROWS), record, jnp.asarray(small), jnp.asarray(forward), jnp.asarray(inverse))


def solution(mesh):
    placed = (P("recv", "tm"), P(), P("recv", "tm"))
    return jax.shard_map(
        local, mesh=mesh, in_specs=placed, out_specs=P("tm", "recv", None), check_vma=False
    )
```

```python
import functools

import jax
import jax.numpy as jnp
import numpy as np
from jax import lax
from jax.experimental import pallas as pl
from jax.experimental.pallas import tpu as pltpu
from jax.sharding import PartitionSpec as P

SEGLEN = 2048
NF = 1024
LAGS = 256
SMOOTH = 64
NSRC = 16
SEGS = 4
ROWS = 16
HALF = 1024
LANES = 128
OWNERS = 8
PLANES = 8
COLS = 4
YROWS = 4
MINE = 4
MESH = pl.DeviceIdType.MESH


def split_bf16(table):
    bf16 = jnp.dtype(jnp.bfloat16)
    high = table.astype(bf16)
    low = (table - high.astype(np.float64)).astype(bf16)
    return high, low


@functools.cache
def tables():
    m = np.arange(16)[:, None]
    lane = np.arange(LANES)[None, :]
    taper = 0.5 - 0.5 * np.cos(2 * np.pi * (m * 128 + lane) / SEGLEN)
    twist = 2 * np.pi * m * lane / SEGLEN
    j = np.arange(8)[:, None]
    freq = j + 8 * (lane // 64) + 16 * (lane % 64)
    counts = np.minimum(freq + SMOOTH, NF - 1) - np.maximum(freq - SMOOTH, 0) + 1
    small = np.concatenate([taper, np.cos(twist), np.sin(twist), 1.0 / counts]).astype(np.float32)

    angle = 2 * np.pi * (np.arange(128)[:, None] * np.arange(64)[None, :] % 128) / 128
    forward = np.zeros((4, 128, 4, 64))
    for h in range(2):
        forward[2 * h, :, h] = np.cos(angle)
        forward[2 * h + 1, :, h] = np.sin(angle)
        forward[2 * h, :, 2 + h] = -np.sin(angle)
        forward[2 * h + 1, :, 2 + h] = np.cos(angle)
    forward = forward.reshape(512, 256)

    lag = np.arange(LAGS)[None, None, :] - LAGS // 2
    turn = 2 * np.pi * (freq[:, :, None] * lag % SEGLEN) / SEGLEN
    factor = np.where(freq == 0, 1.0, 2.0)[:, :, None] / SEGLEN
    inverse = np.stack([factor * np.cos(turn), -factor * np.sin(turn)], axis=1).reshape(2 * NF, LAGS)
    return small, np.stack(split_bf16(forward)), np.stack(split_bf16(inverse))


def halves(x):
    high = x.astype(jnp.bfloat16)
    low = (x - high.astype(jnp.float32)).astype(jnp.bfloat16)
    return high, low


def dot3(high, low, tab_high, tab_low):
    dot = functools.partial(jnp.dot, preferred_element_type=jnp.float32)
    return dot(high, tab_high) + dot(low, tab_high) + dot(high, tab_low)


def real_dft16(x):
    r2 = np.float32(np.sqrt(0.5))
    c1 = np.float32(np.cos(np.pi / 8))
    s1 = np.float32(np.sin(np.pi / 8))
    a = [x[m] + x[m + 8] for m in range(8)]
    b = [x[m] - x[m + 8] for m in range(8)]
    a2 = [a[m] + a[m + 4] for m in range(4)]
    b2 = [a[m] - a[m + 4] for m in range(4)]
    even, odd = a2[0] + a2[2], a2[1] + a2[3]
    out = [None] * 9
    out[0] = (even + odd, None)
    out[8] = (even - odd, None)
    out[4] = (a2[0] - a2[2], a2[3] - a2[1])
    diff, total = r2 * (b2[1] - b2[3]), r2 * (b2[1] + b2[3])
    out[2] = (b2[0] + diff, -(b2[2] + total))
    out[6] = (b2[0] - diff, b2[2] - total)
    u1, u2, u3 = b[1] - b[7], r2 * (b[2] - b[6]), b[3] - b[5]
    v1, v2, v3 = b[1] + b[7], r2 * (b[2] + b[6]), b[3] + b[5]
    up, um = b[0] + u2, b[0] - u2
    vp, vm = v2 + b[4], v2 - b[4]
    p, q = c1 * u1 + s1 * u3, s1 * u1 - c1 * u3
    out[1] = (up + p, -(s1 * v1 + c1 * v3 + vp))
    out[7] = (up - p, -(s1 * v1 + c1 * v3 - vp))
    out[3] = (um + q, -(c1 * v1 - s1 * v3 + vm))
    out[5] = (um - q, -(c1 * v1 - s1 * v3 - vm))
    return out


def whitened(x, small, forward):
    total = x[0]
    for m in range(1, 16):
        total = total + x[m]
    mean = jnp.sum(total, axis=1, keepdims=True) * (1.0 / SEGLEN)
    tapered = [(x[m] - mean) * small[m : m + 1, :] for m in range(16)]
    base = real_dft16(tapered)
    mid = []
    for f in range(16):
        re, im = base[min(f, 16 - f)]
        if im is not None and f > 8:
            im = -im
        cos, sin = small[16 + f : 17 + f, :], small[32 + f : 33 + f, :]
        if f == 0:
            mid.append((re, jnp.zeros_like(re)))
        elif im is None:
            mid.append((re * cos, -(re * sin)))
        else:
            mid.append((re * cos + im * sin, im * cos - re * sin))
    highs, lows = [], []
    for j in range(8):
        parts = [halves(v) for v in (*mid[j], *mid[j + 8])]
        highs.append(jnp.concatenate([p[0] for p in parts], axis=1))
        lows.append(jnp.concatenate([p[1] for p in parts], axis=1))
    spec = dot3(jnp.concatenate(highs, axis=0), jnp.concatenate(lows, axis=0), forward[0], forward[1])
    rows = x[0].shape[0]
    re = [spec[j * rows : (j + 1) * rows, :LANES] for j in range(8)]
    im = [spec[j * rows : (j + 1) * rows, LANES:] for j in range(8)]
    power = [re[j] * re[j] + im[j] * im[j] for j in range(8)]

    lane = lax.broadcasted_iota(jnp.int32, power[0].shape, 1)
    bin_g = lane % 64
    lower = lane < 64
    zero = jnp.zeros_like(power[0])
    ahead, behind = [power[0]], [power[7]]
    for j in range(1, 8):
        ahead.append(ahead[-1] + power[j])
        behind.append(behind[-1] + power[7 - j])
    behind.reverse()
    other = pltpu.roll(ahead[7], 64, 1)
    lower_total = jnp.where(lower, zero, other)
    upper_total = jnp.where(lower, other, zero)
    all_f = jnp.where(lower, ahead[7] + other, zero)
    three = all_f + pltpu.roll(all_f, 1, 1) + pltpu.roll(all_f, 2, 1)
    seven = jnp.where(lower, pltpu.roll(three, 125, 1) + all_f + pltpu.roll(three, 1, 1), zero)
    seven = seven + pltpu.roll(seven, 64, 1)
    out_re, out_im = [], []
    for j in range(8):
        above = jnp.where(bin_g < 60, pltpu.roll(ahead[j] + lower_total, 124, 1), zero)
        below = jnp.where(bin_g >= 4, pltpu.roll(behind[j] + upper_total, 4, 1), zero)
        smoothed = (seven + above + below) * small[48 + j : 49 + j, :]
        scale = lax.rsqrt(smoothed + 1e-06)
        out_re.append(re[j] * scale)
        out_im.append(im[j] * scale)
    return out_re, out_im


def kernel(
    chan_hbm, mask_hbm, rec_hbm, small_hbm, fwd_hbm, inv_hbm, out_ref,
    chan_ref, mask_ref, rec_ref, small_ref, fwd_ref, inv_ref,
    all_ref, val_ref, vsend_ref, send1_ref, recv1_ref, send2_ref, recv2_ref,
    white_ref, src_ref, high_ref, low_ref,
    tab_sem, rec_ssem, rec_rsem, val_ssem, val_rsem, ssem1, rsem1, ssem2, rsem2, ready_sem,
):
    r = lax.axis_index("recv")
    t = lax.axis_index("tm")
    x, yh, z = r % COLS, (r // COLS) % YROWS, r // 16
    line = r - x
    dest = z // 2

    loads = [
        pltpu.make_async_copy(src, dst, tab_sem.at[n])
        for n, (src, dst) in enumerate(
            (
                (rec_hbm, rec_ref),
                (chan_hbm, chan_ref),
                (mask_hbm, mask_ref),
                (small_hbm, small_ref),
                (fwd_hbm, fwd_ref),
                (inv_hbm, inv_ref),
            )
        )
    ]
    for load in loads:
        load.start()

    barrier = pltpu.get_barrier_semaphore()

    def at(plane, row):
        return plane * 16 + row * COLS + x

    def greet(recv, tm):
        pl.semaphore_signal(barrier, inc=1, device_id={"recv": recv, "tm": tm}, device_id_type=MESH)

    for d in range(1, COLS):
        greet(line + (x + d) % COLS, t)
    for d in range(1, SEGS):
        greet(r, (t + d) % SEGS)

    @pl.when(t == dest)
    def _():
        for b in range(SEGS):
            for d in range(1, YROWS):
                greet(at(z, (yh + d) % YROWS), b)

    for p in range(2):

        @pl.when(2 * t + p > z)
        def _(p=p):
            for b in range(SEGS):
                for row in range(YROWS):
                    greet(at(2 * t + p, row), b)

    for target in range(1, PLANES):

        @pl.when(target > z)
        def _(target=target):
            for row in range(YROWS):
                greet(at(target, row), dest)

    for load in loads[:3]:
        load.wait()
    mask = jnp.broadcast_to(mask_ref[...].astype(jnp.float32), (ROWS, ROWS))
    square = (ROWS, ROWS)
    diagonal = lax.broadcasted_iota(jnp.int32, square, 0) == lax.broadcasted_iota(jnp.int32, square, 1)
    mask = jnp.sum(jnp.where(diagonal, mask, 0.0), axis=1, keepdims=True)
    valid = jnp.broadcast_to(mask, (ROWS, LANES))
    vsend_ref[...] = valid
    val_ref[t] = valid

    def owner(source):
        return jnp.clip((chan_ref[source] - source * (OWNERS * ROWS)) // ROWS, 0, OWNERS - 1)

    source = r // OWNERS
    index = jnp.clip(chan_ref[source] - r * ROWS, 0, ROWS - 1)
    picked = rec_ref[pl.ds(index, 1), :]
    for m in range(8):
        piece = picked[:, m * LANES : (m + 1) * LANES]
        send1_ref[pl.ds(m, 1), :] = piece
        recv1_ref[x, pl.ds(m, 1), :] = piece
    piece = vsend_ref[pl.ds(index, 1), :]
    send1_ref[pl.ds(8, 1), :] = piece
    recv1_ref[x, pl.ds(8, 1), :] = piece
    all_ref[t] = rec_ref[...]
    all_ref[SEGS] = jnp.zeros((ROWS, HALF), jnp.float32)

    lower_holders = jnp.clip(z - 2 * t, 0, 2)
    pl.semaphore_wait(barrier, (COLS - 1) + (SEGS - 1) + (YROWS - 1) + YROWS * z + 16 * lower_holders)

    sends = []
    for d in range(1, COLS):
        copy = pltpu.make_async_remote_copy(
            send1_ref, recv1_ref.at[x], ssem1.at[d], rsem1.at[x],
            device_id={"recv": line + (x + d) % COLS, "tm": t}, device_id_type=MESH,
        )
        copy.start()
        sends.append(copy)
    for d in range(1, SEGS):
        to = {"recv": r, "tm": (t + d) % SEGS}
        copy = pltpu.make_async_remote_copy(
            rec_ref, all_ref.at[t], rec_ssem.at[d], rec_rsem.at[t], device_id=to, device_id_type=MESH
        )
        copy.start()
        sends.append(copy)
        copy = pltpu.make_async_remote_copy(
            vsend_ref, val_ref.at[t], val_ssem.at[d], val_rsem.at[t], device_id=to, device_id_type=MESH
        )
        copy.start()
        sends.append(copy)

    for p in range(2):

        @pl.when(2 * t + p < z)
        def _(p=p):
            for b in range(SEGS):
                for row in range(YROWS):
                    pl.semaphore_signal(
                        ready_sem.at[YROWS * z + yh], inc=1,
                        device_id={"recv": at(2 * t + p, row), "tm": b}, device_id_type=MESH,
                    )

    def arrived(buf, sem):
        pltpu.make_async_remote_copy(
            buf, buf, sem, sem, device_id={"recv": r, "tm": t}, device_id_type=MESH
        ).wait_recv()

    for d in range(1, COLS):
        slot = (x + d) % COLS
        arrived(recv1_ref.at[slot], rsem1.at[slot])

    chosen = recv1_ref[owner(source) % COLS]
    send2_ref[...] = chosen
    entry = t * MINE + (z % 2) * 2 + yh // 2

    @pl.when(t == dest)
    def _():
        recv2_ref[yh % 2, entry] = chosen

    def spread(target, row):
        n = YROWS * target + row
        return pltpu.make_async_remote_copy(
            send2_ref, recv2_ref.at[yh % 2, entry], ssem2.at[n], rsem2.at[yh % 2, entry],
            device_id={"recv": at(target, row), "tm": dest}, device_id_type=MESH,
        )

    def apart(target, row):
        return jnp.logical_or(jnp.logical_or(target != z, row != yh), t != dest)

    for target in range(PLANES):
        for row in range(YROWS):
            pl.when(jnp.logical_and(target <= z, apart(target, row)))(spread(target, row).start)

    for d in range(1, SEGS):
        slot = (t + d) % SEGS
        arrived(all_ref.at[slot], rec_rsem.at[slot])
        arrived(val_ref.at[slot], val_rsem.at[slot])
    loads[3].wait()
    loads[4].wait()
    small = small_ref[...]

    @pl.loop(0, SEGS)
    def _(k):
        first, second = all_ref[k], all_ref[k + 1]
        xs = [first[:, m * LANES : (m + 1) * LANES] for m in range(8)]
        xs += [second[:, m * LANES : (m + 1) * LANES] for m in range(8)]
        re, im = whitened(xs, small, (fwd_ref[0], fwd_ref[1]))
        for j in range(8):
            white_ref[k, j, :, :LANES] = re[j]
            white_ref[k, j, :, LANES:] = im[j]

    for target in range(1, PLANES):

        @pl.when(target > z)
        def _(target=target):
            for row in range(YROWS):
                pl.semaphore_wait(ready_sem.at[YROWS * target + row], 1)
                spread(target, row).start()

    for e in range(SEGS * MINE):
        for half in range(2):
            b, p, row = e // MINE, (e % MINE) // 2, 2 * (e % 2) + half
            own = jnp.logical_and(jnp.logical_and(t == b, z == 2 * t + p), yh == row)

            @pl.when(jnp.logical_not(own))
            def _(e=e, half=half):
                arrived(recv2_ref.at[half, e], rsem2.at[half, e])

    turn = lax.broadcasted_iota(jnp.int32, (SEGS * MINE, LANES), 0) % MINE
    upper = jnp.zeros((SEGS * MINE, LANES), jnp.int32)
    for s in range(MINE):
        upper = jnp.where(turn == s, owner(MINE * t + s) // COLS, upper)

    def source_rows(m):
        return jnp.where(upper == 1, recv2_ref[1, :, m, :], recv2_ref[0, :, m, :])

    none = jnp.zeros((MINE, LANES), jnp.float32)
    xs = [source_rows(m) for m in range(8)]
    xs += [jnp.concatenate([v[MINE:], none], axis=0) for v in xs]
    src_valid = source_rows(8)
    re, im = whitened(xs, small, (fwd_ref[0], fwd_ref[1]))
    for j in range(8):
        src_ref[j, :, :LANES] = re[j]
        src_ref[j, :, LANES:] = im[j]

    @pl.loop(0, SEGS)
    def _(k):
        for j in range(8):
            rec_re, rec_im = white_ref[k, j, :, :LANES], white_ref[k, j, :, LANES:]
            for s in range(MINE):
                src = src_ref[j, pl.ds(k * MINE + s, 1), :]
                src_re, src_im = src[:, :LANES], src[:, LANES:]
                cross_re = src_re * rec_re + src_im * rec_im
                cross_im = src_re * rec_im - src_im * rec_re
                rows = pl.ds(pl.multiple_of(k * (MINE * ROWS), MINE * ROWS) + s * ROWS, ROWS)
                for part, value in enumerate((cross_re, cross_im)):
                    high, low = halves(value)
                    first = (2 * j + part) * LANES
                    high_ref[rows, first : first + LANES] = high
                    low_ref[rows, first : first + LANES] = low

    loads[5].wait()
    lag = dot3(high_ref[...], low_ref[...], inv_ref[0], inv_ref[1])
    power = jnp.sum(lag * lag, axis=1, keepdims=True) * (1.0 / LAGS)
    scale = lax.rsqrt(power + 1e-06)
    for s in range(MINE):
        stack = None
        for k in range(SEGS):
            first = (k * MINE + s) * ROWS
            weight = val_ref[k] * src_valid[k * MINE + s : k * MINE + s + 1, :]
            term = lag[first : first + ROWS] * (scale[first : first + ROWS] * weight[:, :1])
            stack = term if stack is None else stack + term
        out_ref[s] = stack

    for copy in sends:
        copy.wait_send()

    for target in range(PLANES):
        for row in range(YROWS):
            pl.when(apart(target, row))(spread(target, row).wait_send)


def local(record, source_channels, valid_mask):
    small, forward, inverse = tables()
    f32, bf16 = jnp.float32, jnp.bfloat16
    vmem = pl.BlockSpec(memory_space=pltpu.VMEM)
    hbm = pl.BlockSpec(memory_space=pltpu.HBM)
    dma = pltpu.SemaphoreType.DMA
    return pl.pallas_call(
        kernel,
        out_shape=jax.ShapeDtypeStruct((MINE, ROWS, LAGS), f32),
        in_specs=[hbm] * 6,
        out_specs=vmem,
        scratch_shapes=[
            pltpu.SMEM((NSRC,), jnp.int32),
            pltpu.VMEM((1, ROWS), jnp.int32),
            pltpu.VMEM((ROWS, HALF), f32),
            pltpu.VMEM(small.shape, f32),
            pltpu.VMEM(forward.shape, bf16),
            pltpu.VMEM(inverse.shape, bf16),
            pltpu.VMEM((SEGS + 1, ROWS, HALF), f32),
            pltpu.VMEM((SEGS, ROWS, LANES), f32),
            pltpu.VMEM((ROWS, LANES), f32),
            pltpu.VMEM((9, LANES), f32),
            pltpu.VMEM((COLS, 9, LANES), f32),
            pltpu.VMEM((9, LANES), f32),
            pltpu.VMEM((2, SEGS * MINE, 9, LANES), f32),
            pltpu.VMEM((SEGS, 8, ROWS, 256), f32),
            pltpu.VMEM((8, SEGS * MINE, 256), f32),
            pltpu.VMEM((SEGS * MINE * ROWS, 2 * NF), bf16),
            pltpu.VMEM((SEGS * MINE * ROWS, 2 * NF), bf16),
            dma((6,)), dma((SEGS,)), dma((SEGS,)), dma((SEGS,)), dma((SEGS,)),
            dma((COLS,)), dma((COLS,)), dma((PLANES * YROWS,)), dma((2, SEGS * MINE)),
            pltpu.SemaphoreType.REGULAR((PLANES * YROWS,)),
        ],
        compiler_params=pltpu.CompilerParams(
            collective_id=0, has_side_effects=True, vmem_limit_bytes=60 * 2**20
        ),
        name="correlate",
    )(source_channels, valid_mask.reshape(1, ROWS), record, jnp.asarray(small), jnp.asarray(forward), jnp.asarray(inverse))


def solution(mesh):
    placed = (P("recv", "tm"), P(), P("recv", "tm"))
    return jax.shard_map(
        local, mesh=mesh, in_specs=placed, out_specs=P("tm", "recv", None), check_vma=False
    )
```

```python
import functools

import jax
import jax.numpy as jnp
import numpy as np
from jax import lax
from jax.experimental import pallas as pl
from jax.experimental.pallas import tpu as pltpu
from jax.sharding import PartitionSpec as P

SEGLEN = 2048
NF = 1024
LAGS = 256
SMOOTH = 64
NSRC = 16
SEGS = 4
ROWS = 16
HALF = 1024
LANES = 128
OWNERS = 8
PLANES = 8
COLS = 4
MINE = 4
MESH = pl.DeviceIdType.MESH


def split_bf16(table):
    bf16 = jnp.dtype(jnp.bfloat16)
    high = table.astype(bf16)
    low = (table - high.astype(np.float64)).astype(bf16)
    return high, low


@functools.cache
def tables():
    m = np.arange(16)[:, None]
    lane = np.arange(LANES)[None, :]
    taper = 0.5 - 0.5 * np.cos(2 * np.pi * (m * 128 + lane) / SEGLEN)
    twist = 2 * np.pi * m * lane / SEGLEN
    j = np.arange(8)[:, None]
    freq = j + 8 * (lane // 64) + 16 * (lane % 64)
    counts = np.minimum(freq + SMOOTH, NF - 1) - np.maximum(freq - SMOOTH, 0) + 1
    small = np.concatenate([taper, np.cos(twist), np.sin(twist), 1.0 / counts]).astype(np.float32)

    angle = 2 * np.pi * (np.arange(128)[:, None] * np.arange(64)[None, :] % 128) / 128
    forward = np.zeros((4, 128, 4, 64))
    for h in range(2):
        forward[2 * h, :, h] = np.cos(angle)
        forward[2 * h + 1, :, h] = np.sin(angle)
        forward[2 * h, :, 2 + h] = -np.sin(angle)
        forward[2 * h + 1, :, 2 + h] = np.cos(angle)
    forward = forward.reshape(512, 256)

    lag = np.arange(LAGS)[None, None, :] - LAGS // 2
    turn = 2 * np.pi * (freq[:, :, None] * lag % SEGLEN) / SEGLEN
    factor = np.where(freq == 0, 1.0, 2.0)[:, :, None] / SEGLEN
    inverse = np.stack([factor * np.cos(turn), -factor * np.sin(turn)], axis=1).reshape(2 * NF, LAGS)
    return small, np.stack(split_bf16(forward)), np.stack(split_bf16(inverse))


def halves(x):
    high = x.astype(jnp.bfloat16)
    low = (x - high.astype(jnp.float32)).astype(jnp.bfloat16)
    return high, low


def dot3(high, low, tab_high, tab_low):
    dot = functools.partial(jnp.dot, preferred_element_type=jnp.float32)
    return dot(high, tab_high) + dot(low, tab_high) + dot(high, tab_low)


def real_dft16(x):
    r2 = np.float32(np.sqrt(0.5))
    c1 = np.float32(np.cos(np.pi / 8))
    s1 = np.float32(np.sin(np.pi / 8))
    a = [x[m] + x[m + 8] for m in range(8)]
    b = [x[m] - x[m + 8] for m in range(8)]
    a2 = [a[m] + a[m + 4] for m in range(4)]
    b2 = [a[m] - a[m + 4] for m in range(4)]
    even, odd = a2[0] + a2[2], a2[1] + a2[3]
    out = [None] * 9
    out[0] = (even + odd, None)
    out[8] = (even - odd, None)
    out[4] = (a2[0] - a2[2], a2[3] - a2[1])
    diff, total = r2 * (b2[1] - b2[3]), r2 * (b2[1] + b2[3])
    out[2] = (b2[0] + diff, -(b2[2] + total))
    out[6] = (b2[0] - diff, b2[2] - total)
    u1, u2, u3 = b[1] - b[7], r2 * (b[2] - b[6]), b[3] - b[5]
    v1, v2, v3 = b[1] + b[7], r2 * (b[2] + b[6]), b[3] + b[5]
    up, um = b[0] + u2, b[0] - u2
    vp, vm = v2 + b[4], v2 - b[4]
    p, q = c1 * u1 + s1 * u3, s1 * u1 - c1 * u3
    out[1] = (up + p, -(s1 * v1 + c1 * v3 + vp))
    out[7] = (up - p, -(s1 * v1 + c1 * v3 - vp))
    out[3] = (um + q, -(c1 * v1 - s1 * v3 + vm))
    out[5] = (um - q, -(c1 * v1 - s1 * v3 - vm))
    return out


def whitened(x, small, forward):
    total = x[0]
    for m in range(1, 16):
        total = total + x[m]
    mean = jnp.sum(total, axis=1, keepdims=True) * (1.0 / SEGLEN)
    tapered = [(x[m] - mean) * small[m : m + 1, :] for m in range(16)]
    base = real_dft16(tapered)
    mid = []
    for f in range(16):
        re, im = base[min(f, 16 - f)]
        if im is not None and f > 8:
            im = -im
        cos, sin = small[16 + f : 17 + f, :], small[32 + f : 33 + f, :]
        if f == 0:
            mid.append((re, jnp.zeros_like(re)))
        elif im is None:
            mid.append((re * cos, -(re * sin)))
        else:
            mid.append((re * cos + im * sin, im * cos - re * sin))
    highs, lows = [], []
    for j in range(8):
        parts = [halves(v) for v in (*mid[j], *mid[j + 8])]
        highs.append(jnp.concatenate([p[0] for p in parts], axis=1))
        lows.append(jnp.concatenate([p[1] for p in parts], axis=1))
    spec = dot3(jnp.concatenate(highs, axis=0), jnp.concatenate(lows, axis=0), forward[0], forward[1])
    rows = x[0].shape[0]
    re = [spec[j * rows : (j + 1) * rows, :LANES] for j in range(8)]
    im = [spec[j * rows : (j + 1) * rows, LANES:] for j in range(8)]
    power = [re[j] * re[j] + im[j] * im[j] for j in range(8)]

    lane = lax.broadcasted_iota(jnp.int32, power[0].shape, 1)
    bin_g = lane % 64
    lower = lane < 64
    zero = jnp.zeros_like(power[0])
    ahead, behind = [power[0]], [power[7]]
    for j in range(1, 8):
        ahead.append(ahead[-1] + power[j])
        behind.append(behind[-1] + power[7 - j])
    behind.reverse()
    other = pltpu.roll(ahead[7], 64, 1)
    lower_total = jnp.where(lower, zero, other)
    upper_total = jnp.where(lower, other, zero)
    all_f = jnp.where(lower, ahead[7] + other, zero)
    three = all_f + pltpu.roll(all_f, 1, 1) + pltpu.roll(all_f, 2, 1)
    seven = jnp.where(lower, pltpu.roll(three, 125, 1) + all_f + pltpu.roll(three, 1, 1), zero)
    seven = seven + pltpu.roll(seven, 64, 1)
    out_re, out_im = [], []
    for j in range(8):
        above = jnp.where(bin_g < 60, pltpu.roll(ahead[j] + lower_total, 124, 1), zero)
        below = jnp.where(bin_g >= 4, pltpu.roll(behind[j] + upper_total, 4, 1), zero)
        smoothed = (seven + above + below) * small[48 + j : 49 + j, :]
        scale = lax.rsqrt(smoothed + 1e-06)
        out_re.append(re[j] * scale)
        out_im.append(im[j] * scale)
    return out_re, out_im


def kernel(
    chan_hbm, mask_hbm, rec_hbm, small_hbm, fwd_hbm, inv_hbm, out_ref,
    chan_ref, mask_ref, rec_ref, small_ref, fwd_ref, inv_ref, all_ref, val_ref, vsend_ref, send1_ref, recv1_ref, send2_ref, recv2_ref,
    white_ref, src_ref, high_ref, low_ref,
    tab_sem, rec_ssem, rec_rsem, val_ssem, val_rsem, ssem1, rsem1, ssem2, rsem2, ready_sem,
):
    r = lax.axis_index("recv")
    t = lax.axis_index("tm")
    x, yh, z = r % COLS, (r // COLS) % 4, r // 16
    cand = r % OWNERS
    group = r // OWNERS
    dest = z // 2

    loads = [
        pltpu.make_async_copy(src, dst, tab_sem.at[n])
        for n, (src, dst) in enumerate(
            (
                (rec_hbm, rec_ref),
                (chan_hbm, chan_ref),
                (mask_hbm, mask_ref),
                (small_hbm, small_ref),
                (fwd_hbm, fwd_ref),
                (inv_hbm, inv_ref),
            )
        )
    ]
    for load in loads:
        load.start()

    barrier = pltpu.get_barrier_semaphore()

    def greet(recv, tm):
        pl.semaphore_signal(barrier, inc=1, device_id={"recv": recv, "tm": tm}, device_id_type=MESH)

    rows = (yh, 3 - yh)
    for d in range(1, OWNERS):
        greet(group * OWNERS + (cand + d) % OWNERS, t)
    for d in range(1, SEGS):
        greet(r, (t + d) % SEGS)

    @pl.when(t == dest)
    def _():
        for b in range(SEGS):
            greet(z * 16 + rows[1] * COLS + x, b)

    for p in range(2):

        @pl.when(2 * t + p > z)
        def _(p=p):
            for b in range(SEGS):
                for row in rows:
                    greet((2 * t + p) * 16 + row * COLS + x, b)

    for target in range(1, PLANES):

        @pl.when(target > z)
        def _(target=target):
            for row in rows:
                greet(target * 16 + row * COLS + x, dest)

    for load in loads[:3]:
        load.wait()
    rec = rec_ref[...]
    mask = jnp.broadcast_to(mask_ref[...].astype(jnp.float32), (ROWS, ROWS))
    square = (ROWS, ROWS)
    diagonal = lax.broadcasted_iota(jnp.int32, square, 0) == lax.broadcasted_iota(jnp.int32, square, 1)
    mask = jnp.sum(jnp.where(diagonal, mask, 0.0), axis=1, keepdims=True)
    valid = jnp.broadcast_to(mask, (ROWS, LANES))
    vsend_ref[...] = valid
    val_ref[t] = valid
    all_ref[t] = rec
    all_ref[SEGS] = jnp.zeros((ROWS, HALF), jnp.float32)

    index = jnp.clip(chan_ref[group] - r * ROWS, 0, ROWS - 1)
    picked = rec_ref[pl.ds(index, 1), :]
    for m in range(8):
        piece = picked[:, m * LANES : (m + 1) * LANES]
        send1_ref[pl.ds(m, 1), :] = piece
        recv1_ref[cand, pl.ds(m, 1), :] = piece
    piece = vsend_ref[pl.ds(index, 1), :]
    send1_ref[pl.ds(8, 1), :] = piece
    recv1_ref[cand, pl.ds(8, 1), :] = piece

    lower_holders = jnp.clip(z - 2 * t, 0, 2)
    pl.semaphore_wait(barrier, (OWNERS - 1) + (SEGS - 1) + 1 + 2 * z + 8 * lower_holders)

    for p in range(2):

        @pl.when(2 * t + p < z)
        def _(p=p):
            for b in range(SEGS):
                for flip, row in enumerate(rows):
                    pl.semaphore_signal(
                        ready_sem.at[2 * z + flip], inc=1,
                        device_id={"recv": (2 * t + p) * 16 + row * COLS + x, "tm": b}, device_id_type=MESH,
                    )

    sends = []
    for d in range(1, OWNERS):
        copy = pltpu.make_async_remote_copy(
            send1_ref, recv1_ref.at[cand], ssem1.at[d], rsem1.at[cand],
            device_id={"recv": group * OWNERS + (cand + d) % OWNERS, "tm": t}, device_id_type=MESH,
        )
        copy.start()
        sends.append(copy)
    for d in range(1, SEGS):
        to = {"recv": r, "tm": (t + d) % SEGS}
        copy = pltpu.make_async_remote_copy(
            rec_ref, all_ref.at[t], rec_ssem.at[d], rec_rsem.at[t], device_id=to, device_id_type=MESH
        )
        copy.start()
        sends.append(copy)
        copy = pltpu.make_async_remote_copy(
            vsend_ref, val_ref.at[t], val_ssem.at[d], val_rsem.at[t], device_id=to, device_id_type=MESH
        )
        copy.start()
        sends.append(copy)

    def arrived(buf, sem):
        pltpu.make_async_remote_copy(
            buf, buf, sem, sem, device_id={"recv": r, "tm": t}, device_id_type=MESH
        ).wait_recv()

    for d in range(1, OWNERS):
        slot = (cand + d) % OWNERS
        arrived(recv1_ref.at[slot], rsem1.at[slot])

    owner = jnp.clip((chan_ref[group] - group * (OWNERS * ROWS)) // ROWS, 0, OWNERS - 1)
    chosen = recv1_ref[owner]
    send2_ref[...] = chosen
    entry = t * MINE + (z % 2) * 2 + yh // 2

    @pl.when(t == dest)
    def _():
        recv2_ref[entry] = chosen

    def spread(target, flip):
        return pltpu.make_async_remote_copy(
            send2_ref, recv2_ref.at[entry], ssem2.at[2 * target + flip], rsem2.at[entry],
            device_id={"recv": target * 16 + rows[flip] * COLS + x, "tm": dest}, device_id_type=MESH,
        )

    for target in range(PLANES):
        pl.when(target <= z)(spread(target, 1).start)
        pl.when(jnp.logical_or(target < z, jnp.logical_and(target == z, t != dest)))(spread(target, 0).start)

    for d in range(1, SEGS):
        slot = (t + d) % SEGS
        arrived(all_ref.at[slot], rec_rsem.at[slot])
        arrived(val_ref.at[slot], val_rsem.at[slot])
    loads[3].wait()
    loads[4].wait()
    small = small_ref[...]

    @pl.loop(0, SEGS)
    def _(k):
        first, second = all_ref[k], all_ref[k + 1]
        xs = [first[:, m * LANES : (m + 1) * LANES] for m in range(8)]
        xs += [second[:, m * LANES : (m + 1) * LANES] for m in range(8)]
        re, im = whitened(xs, small, (fwd_ref[0], fwd_ref[1]))
        for j in range(8):
            white_ref[k, j, :, :LANES] = re[j]
            white_ref[k, j, :, LANES:] = im[j]

    for target in range(1, PLANES):

        @pl.when(target > z)
        def _(target=target):
            for flip in range(2):
                pl.semaphore_wait(ready_sem.at[2 * target + flip], 1)
                spread(target, flip).start()

    for e in range(SEGS * MINE):
        b, p, h = e // MINE, (e % MINE) // 2, e % 2
        own = jnp.logical_and(jnp.logical_and(t == b, z == 2 * t + p), yh // 2 == h)

        @pl.when(jnp.logical_not(own))
        def _(e=e):
            arrived(recv2_ref.at[e], rsem2.at[e])

    none = jnp.zeros((MINE, LANES), jnp.float32)
    xs = [recv2_ref[:, m, :] for m in range(8)]
    xs += [jnp.concatenate([v[MINE:], none], axis=0) for v in xs]
    re, im = whitened(xs, small, (fwd_ref[0], fwd_ref[1]))
    for j in range(8):
        src_ref[j, :, :LANES] = re[j]
        src_ref[j, :, LANES:] = im[j]

    @pl.loop(0, SEGS)
    def _(k):
        for j in range(8):
            rec_re, rec_im = white_ref[k, j, :, :LANES], white_ref[k, j, :, LANES:]
            for s in range(MINE):
                src = src_ref[j, pl.ds(k * MINE + s, 1), :]
                src_re, src_im = src[:, :LANES], src[:, LANES:]
                cross_re = src_re * rec_re + src_im * rec_im
                cross_im = src_re * rec_im - src_im * rec_re
                rows = pl.ds(pl.multiple_of(k * (MINE * ROWS), MINE * ROWS) + s * ROWS, ROWS)
                for part, value in enumerate((cross_re, cross_im)):
                    high, low = halves(value)
                    first = (2 * j + part) * LANES
                    high_ref[rows, first : first + LANES] = high
                    low_ref[rows, first : first + LANES] = low

    loads[5].wait()
    lag = dot3(high_ref[...], low_ref[...], inv_ref[0], inv_ref[1])
    power = jnp.sum(lag * lag, axis=1, keepdims=True) * (1.0 / LAGS)
    scale = lax.rsqrt(power + 1e-06)
    for s in range(MINE):
        stack = None
        for k in range(SEGS):
            first = (k * MINE + s) * ROWS
            weight = val_ref[k] * recv2_ref[k * MINE + s, pl.ds(8, 1), :]
            term = lag[first : first + ROWS] * (scale[first : first + ROWS] * weight[:, :1])
            stack = term if stack is None else stack + term
        out_ref[s] = stack

    for copy in sends:
        copy.wait_send()

    for target in range(PLANES):
        spread(target, 1).wait_send()
        pl.when(jnp.logical_or(target != z, t != dest))(spread(target, 0).wait_send)


def local(record, source_channels, valid_mask):
    small, forward, inverse = tables()
    f32, bf16 = jnp.float32, jnp.bfloat16
    vmem = pl.BlockSpec(memory_space=pltpu.VMEM)
    hbm = pl.BlockSpec(memory_space=pltpu.HBM)
    dma = pltpu.SemaphoreType.DMA
    return pl.pallas_call(
        kernel,
        out_shape=pltpu.VMEM((MINE, ROWS, LAGS), f32),
        in_specs=[hbm] * 6,
        out_specs=vmem,
        scratch_shapes=[
            pltpu.SMEM((NSRC,), jnp.int32),
            pltpu.VMEM((1, ROWS), jnp.int32),
            pltpu.VMEM((ROWS, HALF), f32),
            pltpu.VMEM(small.shape, f32),
            pltpu.VMEM(forward.shape, bf16),
            pltpu.VMEM(inverse.shape, bf16),
            pltpu.VMEM((SEGS + 1, ROWS, HALF), f32),
            pltpu.VMEM((SEGS, ROWS, LANES), f32),
            pltpu.VMEM((ROWS, LANES), f32),
            pltpu.VMEM((9, LANES), f32),
            pltpu.VMEM((OWNERS, 9, LANES), f32),
            pltpu.VMEM((9, LANES), f32),
            pltpu.VMEM((SEGS * MINE, 9, LANES), f32),
            pltpu.VMEM((SEGS, 8, ROWS, 256), f32),
            pltpu.VMEM((8, SEGS * MINE, 256), f32),
            pltpu.VMEM((SEGS * MINE * ROWS, 2 * NF), bf16),
            pltpu.VMEM((SEGS * MINE * ROWS, 2 * NF), bf16),
            dma((6,)), dma((SEGS,)), dma((SEGS,)), dma((SEGS,)), dma((SEGS,)),
            dma((OWNERS,)), dma((OWNERS,)), dma((16,)), dma((16,)), pltpu.SemaphoreType.REGULAR((16,)),
        ],
        compiler_params=pltpu.CompilerParams(
            collective_id=0, has_side_effects=True, vmem_limit_bytes=60 * 2**20
        ),
        name="correlate",
    )(source_channels, valid_mask.reshape(1, ROWS), record, jnp.asarray(small), jnp.asarray(forward), jnp.asarray(inverse))


def solution(mesh):
    placed = (P("recv", "tm"), P(), P("recv", "tm"))
    return jax.shard_map(
        local, mesh=mesh, in_specs=placed, out_specs=P("tm", "recv", None), check_vma=False
    )
```

```python
import functools

import jax
import jax.numpy as jnp
import numpy as np
from jax import lax
from jax.experimental import pallas as pl
from jax.experimental.pallas import tpu as pltpu
from jax.sharding import PartitionSpec as P

SEGLEN = 2048
NF = 1024
LAGS = 256
SMOOTH = 64
NSRC = 16
SEGS = 4
ROWS = 16
HALF = 1024
LANES = 128
OWNERS = 8
PLANES = 8
COLS = 4
MINE = 4
MESH = pl.DeviceIdType.MESH


def split_bf16(table):
    bf16 = jnp.dtype(jnp.bfloat16)
    high = table.astype(bf16)
    low = (table - high.astype(np.float64)).astype(bf16)
    return high, low


@functools.cache
def tables():
    m = np.arange(16)[:, None]
    lane = np.arange(LANES)[None, :]
    taper = 0.5 - 0.5 * np.cos(2 * np.pi * (m * 128 + lane) / SEGLEN)
    twist = 2 * np.pi * m * lane / SEGLEN
    j = np.arange(8)[:, None]
    freq = j + 8 * (lane // 64) + 16 * (lane % 64)
    counts = np.minimum(freq + SMOOTH, NF - 1) - np.maximum(freq - SMOOTH, 0) + 1
    small = np.concatenate([taper, np.cos(twist), np.sin(twist), 1.0 / counts]).astype(np.float32)

    angle = 2 * np.pi * (np.arange(128)[:, None] * np.arange(64)[None, :] % 128) / 128
    forward = np.zeros((4, 128, 4, 64))
    for h in range(2):
        forward[2 * h, :, h] = np.cos(angle)
        forward[2 * h + 1, :, h] = np.sin(angle)
        forward[2 * h, :, 2 + h] = -np.sin(angle)
        forward[2 * h + 1, :, 2 + h] = np.cos(angle)
    forward = forward.reshape(512, 256)

    lag = np.arange(LAGS)[None, None, :] - LAGS // 2
    turn = 2 * np.pi * (freq[:, :, None] * lag % SEGLEN) / SEGLEN
    factor = np.where(freq == 0, 1.0, 2.0)[:, :, None] / SEGLEN
    inverse = np.stack([factor * np.cos(turn), -factor * np.sin(turn)], axis=1).reshape(2 * NF, LAGS)
    return small, np.stack(split_bf16(forward)), np.stack(split_bf16(inverse))


def halves(x):
    high = x.astype(jnp.bfloat16)
    low = (x - high.astype(jnp.float32)).astype(jnp.bfloat16)
    return high, low


def dot3(high, low, tab_high, tab_low):
    dot = functools.partial(jnp.dot, preferred_element_type=jnp.float32)
    return dot(high, tab_high) + dot(low, tab_high) + dot(high, tab_low)


def real_dft16(x):
    r2 = np.float32(np.sqrt(0.5))
    c1 = np.float32(np.cos(np.pi / 8))
    s1 = np.float32(np.sin(np.pi / 8))
    a = [x[m] + x[m + 8] for m in range(8)]
    b = [x[m] - x[m + 8] for m in range(8)]
    a2 = [a[m] + a[m + 4] for m in range(4)]
    b2 = [a[m] - a[m + 4] for m in range(4)]
    even, odd = a2[0] + a2[2], a2[1] + a2[3]
    out = [None] * 9
    out[0] = (even + odd, None)
    out[8] = (even - odd, None)
    out[4] = (a2[0] - a2[2], a2[3] - a2[1])
    diff, total = r2 * (b2[1] - b2[3]), r2 * (b2[1] + b2[3])
    out[2] = (b2[0] + diff, -(b2[2] + total))
    out[6] = (b2[0] - diff, b2[2] - total)
    u1, u2, u3 = b[1] - b[7], r2 * (b[2] - b[6]), b[3] - b[5]
    v1, v2, v3 = b[1] + b[7], r2 * (b[2] + b[6]), b[3] + b[5]
    up, um = b[0] + u2, b[0] - u2
    vp, vm = v2 + b[4], v2 - b[4]
    p, q = c1 * u1 + s1 * u3, s1 * u1 - c1 * u3
    out[1] = (up + p, -(s1 * v1 + c1 * v3 + vp))
    out[7] = (up - p, -(s1 * v1 + c1 * v3 - vp))
    out[3] = (um + q, -(c1 * v1 - s1 * v3 + vm))
    out[5] = (um - q, -(c1 * v1 - s1 * v3 - vm))
    return out


def whitened(x, small, forward):
    total = x[0]
    for m in range(1, 16):
        total = total + x[m]
    mean = jnp.sum(total, axis=1, keepdims=True) * (1.0 / SEGLEN)
    tapered = [(x[m] - mean) * small[m : m + 1, :] for m in range(16)]
    base = real_dft16(tapered)
    mid = []
    for f in range(16):
        re, im = base[min(f, 16 - f)]
        if im is not None and f > 8:
            im = -im
        cos, sin = small[16 + f : 17 + f, :], small[32 + f : 33 + f, :]
        if f == 0:
            mid.append((re, jnp.zeros_like(re)))
        elif im is None:
            mid.append((re * cos, -(re * sin)))
        else:
            mid.append((re * cos + im * sin, im * cos - re * sin))
    highs, lows = [], []
    for j in range(8):
        parts = [halves(v) for v in (*mid[j], *mid[j + 8])]
        highs.append(jnp.concatenate([p[0] for p in parts], axis=1))
        lows.append(jnp.concatenate([p[1] for p in parts], axis=1))
    spec = dot3(jnp.concatenate(highs, axis=0), jnp.concatenate(lows, axis=0), forward[0], forward[1])
    rows = x[0].shape[0]
    re = [spec[j * rows : (j + 1) * rows, :LANES] for j in range(8)]
    im = [spec[j * rows : (j + 1) * rows, LANES:] for j in range(8)]
    power = [re[j] * re[j] + im[j] * im[j] for j in range(8)]

    lane = lax.broadcasted_iota(jnp.int32, power[0].shape, 1)
    bin_g = lane % 64
    lower = lane < 64
    zero = jnp.zeros_like(power[0])
    ahead, behind = [power[0]], [power[7]]
    for j in range(1, 8):
        ahead.append(ahead[-1] + power[j])
        behind.append(behind[-1] + power[7 - j])
    behind.reverse()
    other = pltpu.roll(ahead[7], 64, 1)
    lower_total = jnp.where(lower, zero, other)
    upper_total = jnp.where(lower, other, zero)
    all_f = jnp.where(lower, ahead[7] + other, zero)
    three = all_f + pltpu.roll(all_f, 1, 1) + pltpu.roll(all_f, 2, 1)
    seven = jnp.where(lower, pltpu.roll(three, 125, 1) + all_f + pltpu.roll(three, 1, 1), zero)
    seven = seven + pltpu.roll(seven, 64, 1)
    out_re, out_im = [], []
    for j in range(8):
        above = jnp.where(bin_g < 60, pltpu.roll(ahead[j] + lower_total, 124, 1), zero)
        below = jnp.where(bin_g >= 4, pltpu.roll(behind[j] + upper_total, 4, 1), zero)
        smoothed = (seven + above + below) * small[48 + j : 49 + j, :]
        scale = lax.rsqrt(smoothed + 1e-06)
        out_re.append(re[j] * scale)
        out_im.append(im[j] * scale)
    return out_re, out_im


def kernel(
    chan_hbm, mask_hbm, rec_hbm, small_hbm, fwd_hbm, inv_hbm, out_ref,
    chan_ref, mask_ref, rec_ref, small_ref, fwd_ref, inv_ref, all_ref, val_ref, vsend_ref, send1_ref, recv1_ref, send2_ref, recv2_ref,
    white_ref, src_ref,
    tab_sem, rec_ssem, rec_rsem, val_ssem, val_rsem, ssem1, rsem1, ssem2, rsem2, ready_sem,
):
    r = lax.axis_index("recv")
    t = lax.axis_index("tm")
    x, yh, z = r % COLS, (r // COLS) % 4, r // 16
    cand = r % OWNERS
    group = r // OWNERS
    dest = z // 2

    loads = [
        pltpu.make_async_copy(src, dst, tab_sem.at[n])
        for n, (src, dst) in enumerate(
            (
                (rec_hbm, rec_ref),
                (chan_hbm, chan_ref),
                (mask_hbm, mask_ref),
                (small_hbm, small_ref),
                (fwd_hbm, fwd_ref),
                (inv_hbm, inv_ref),
            )
        )
    ]
    for load in loads:
        load.start()

    barrier = pltpu.get_barrier_semaphore()

    def greet(recv, tm):
        pl.semaphore_signal(barrier, inc=1, device_id={"recv": recv, "tm": tm}, device_id_type=MESH)

    rows = (yh, 3 - yh)
    for d in range(1, OWNERS):
        greet(group * OWNERS + (cand + d) % OWNERS, t)
    for d in range(1, SEGS):
        greet(r, (t + d) % SEGS)

    @pl.when(t == dest)
    def _():
        for b in range(SEGS):
            greet(z * 16 + rows[1] * COLS + x, b)

    for p in range(2):

        @pl.when(2 * t + p > z)
        def _(p=p):
            for b in range(SEGS):
                for row in rows:
                    greet((2 * t + p) * 16 + row * COLS + x, b)

    for target in range(1, PLANES):

        @pl.when(target > z)
        def _(target=target):
            for row in rows:
                greet(target * 16 + row * COLS + x, dest)

    for load in loads[:3]:
        load.wait()
    rec = rec_ref[...]
    mask = jnp.broadcast_to(mask_ref[...].astype(jnp.float32), (ROWS, ROWS))
    square = (ROWS, ROWS)
    diagonal = lax.broadcasted_iota(jnp.int32, square, 0) == lax.broadcasted_iota(jnp.int32, square, 1)
    mask = jnp.sum(jnp.where(diagonal, mask, 0.0), axis=1, keepdims=True)
    valid = jnp.broadcast_to(mask, (ROWS, LANES))
    vsend_ref[...] = valid
    val_ref[t] = valid
    all_ref[t] = rec
    all_ref[SEGS] = jnp.zeros((ROWS, HALF), jnp.float32)

    index = jnp.clip(chan_ref[group] - r * ROWS, 0, ROWS - 1)
    picked = rec_ref[pl.ds(index, 1), :]
    for m in range(8):
        piece = picked[:, m * LANES : (m + 1) * LANES]
        send1_ref[pl.ds(m, 1), :] = piece
        recv1_ref[cand, pl.ds(m, 1), :] = piece
    piece = vsend_ref[pl.ds(index, 1), :]
    send1_ref[pl.ds(8, 1), :] = piece
    recv1_ref[cand, pl.ds(8, 1), :] = piece

    lower_holders = jnp.clip(z - 2 * t, 0, 2)
    pl.semaphore_wait(barrier, (OWNERS - 1) + (SEGS - 1) + 1 + 2 * z + 8 * lower_holders)

    for p in range(2):

        @pl.when(2 * t + p < z)
        def _(p=p):
            for b in range(SEGS):
                for flip, row in enumerate(rows):
                    pl.semaphore_signal(
                        ready_sem.at[2 * z + flip], inc=1,
                        device_id={"recv": (2 * t + p) * 16 + row * COLS + x, "tm": b}, device_id_type=MESH,
                    )

    sends = []
    for d in range(1, OWNERS):
        copy = pltpu.make_async_remote_copy(
            send1_ref, recv1_ref.at[cand], ssem1.at[d], rsem1.at[cand],
            device_id={"recv": group * OWNERS + (cand + d) % OWNERS, "tm": t}, device_id_type=MESH,
        )
        copy.start()
        sends.append(copy)
    for d in range(1, SEGS):
        to = {"recv": r, "tm": (t + d) % SEGS}
        copy = pltpu.make_async_remote_copy(
            rec_ref, all_ref.at[t], rec_ssem.at[d], rec_rsem.at[t], device_id=to, device_id_type=MESH
        )
        copy.start()
        sends.append(copy)
        copy = pltpu.make_async_remote_copy(
            vsend_ref, val_ref.at[t], val_ssem.at[d], val_rsem.at[t], device_id=to, device_id_type=MESH
        )
        copy.start()
        sends.append(copy)

    def arrived(buf, sem):
        pltpu.make_async_remote_copy(
            buf, buf, sem, sem, device_id={"recv": r, "tm": t}, device_id_type=MESH
        ).wait_recv()

    for d in range(1, OWNERS):
        slot = (cand + d) % OWNERS
        arrived(recv1_ref.at[slot], rsem1.at[slot])

    owner = jnp.clip((chan_ref[group] - group * (OWNERS * ROWS)) // ROWS, 0, OWNERS - 1)
    chosen = recv1_ref[owner]
    send2_ref[...] = chosen
    entry = t * MINE + (z % 2) * 2 + yh // 2

    @pl.when(t == dest)
    def _():
        recv2_ref[entry] = chosen

    def spread(target, flip):
        return pltpu.make_async_remote_copy(
            send2_ref, recv2_ref.at[entry], ssem2.at[2 * target + flip], rsem2.at[entry],
            device_id={"recv": target * 16 + rows[flip] * COLS + x, "tm": dest}, device_id_type=MESH,
        )

    for target in range(PLANES):
        pl.when(target <= z)(spread(target, 1).start)
        pl.when(jnp.logical_or(target < z, jnp.logical_and(target == z, t != dest)))(spread(target, 0).start)

    for d in range(1, SEGS):
        slot = (t + d) % SEGS
        arrived(all_ref.at[slot], rec_rsem.at[slot])
        arrived(val_ref.at[slot], val_rsem.at[slot])
    loads[3].wait()
    loads[4].wait()
    small = small_ref[...]

    @pl.loop(0, SEGS)
    def _(k):
        first, second = all_ref[k], all_ref[k + 1]
        xs = [first[:, m * LANES : (m + 1) * LANES] for m in range(8)]
        xs += [second[:, m * LANES : (m + 1) * LANES] for m in range(8)]
        re, im = whitened(xs, small, (fwd_ref[0], fwd_ref[1]))
        for j in range(8):
            white_ref[k, j, :, :LANES] = re[j]
            white_ref[k, j, :, LANES:] = im[j]

    for target in range(1, PLANES):

        @pl.when(target > z)
        def _(target=target):
            for flip in range(2):
                pl.semaphore_wait(ready_sem.at[2 * target + flip], 1)
                spread(target, flip).start()

    for e in range(SEGS * MINE):
        b, p, h = e // MINE, (e % MINE) // 2, e % 2
        own = jnp.logical_and(jnp.logical_and(t == b, z == 2 * t + p), yh // 2 == h)

        @pl.when(jnp.logical_not(own))
        def _(e=e):
            arrived(recv2_ref.at[e], rsem2.at[e])

    none = jnp.zeros((MINE, LANES), jnp.float32)
    xs = [recv2_ref[:, m, :] for m in range(8)]
    xs += [jnp.concatenate([v[MINE:], none], axis=0) for v in xs]
    re, im = whitened(xs, small, (fwd_ref[0], fwd_ref[1]))
    for j in range(8):
        src_ref[j, :, :LANES] = re[j]
        src_ref[j, :, LANES:] = im[j]

    def cross(j):
        highs, lows = [], []
        for k in range(SEGS):
            rec_re, rec_im = white_ref[k, j, :, :LANES], white_ref[k, j, :, LANES:]
            for s in range(MINE):
                src = src_ref[j, pl.ds(k * MINE + s, 1), :]
                src_re, src_im = src[:, :LANES], src[:, LANES:]
                parts = halves(src_re * rec_re + src_im * rec_im), halves(src_re * rec_im - src_im * rec_re)
                highs.append(jnp.concatenate([p[0] for p in parts], axis=1))
                lows.append(jnp.concatenate([p[1] for p in parts], axis=1))
        return jnp.concatenate(highs, axis=0), jnp.concatenate(lows, axis=0)

    loads[5].wait()
    lag = None
    for j in range(8):
        high, low = cross(j)
        block = pl.ds(j * 256, 256)
        term = dot3(high, low, inv_ref[0, block, :], inv_ref[1, block, :])
        lag = term if lag is None else lag + term
    power = jnp.sum(lag * lag, axis=1, keepdims=True) * (1.0 / LAGS)
    scale = lax.rsqrt(power + 1e-06)
    for s in range(MINE):
        stack = None
        for k in range(SEGS):
            first = (k * MINE + s) * ROWS
            weight = val_ref[k] * recv2_ref[k * MINE + s, pl.ds(8, 1), :]
            term = lag[first : first + ROWS] * (scale[first : first + ROWS] * weight[:, :1])
            stack = term if stack is None else stack + term
        out_ref[s] = stack

    for copy in sends:
        copy.wait_send()

    for target in range(PLANES):
        spread(target, 1).wait_send()
        pl.when(jnp.logical_or(target != z, t != dest))(spread(target, 0).wait_send)


def local(record, source_channels, valid_mask):
    small, forward, inverse = tables()
    f32, bf16 = jnp.float32, jnp.bfloat16
    vmem = pl.BlockSpec(memory_space=pltpu.VMEM)
    hbm = pl.BlockSpec(memory_space=pltpu.HBM)
    dma = pltpu.SemaphoreType.DMA
    return pl.pallas_call(
        kernel,
        out_shape=pltpu.VMEM((MINE, ROWS, LAGS), f32),
        in_specs=[hbm] * 6,
        out_specs=vmem,
        scratch_shapes=[
            pltpu.SMEM((NSRC,), jnp.int32),
            pltpu.VMEM((1, ROWS), jnp.int32),
            pltpu.VMEM((ROWS, HALF), f32),
            pltpu.VMEM(small.shape, f32),
            pltpu.VMEM(forward.shape, bf16),
            pltpu.VMEM(inverse.shape, bf16),
            pltpu.VMEM((SEGS + 1, ROWS, HALF), f32),
            pltpu.VMEM((SEGS, ROWS, LANES), f32),
            pltpu.VMEM((ROWS, LANES), f32),
            pltpu.VMEM((9, LANES), f32),
            pltpu.VMEM((OWNERS, 9, LANES), f32),
            pltpu.VMEM((9, LANES), f32),
            pltpu.VMEM((SEGS * MINE, 9, LANES), f32),
            pltpu.VMEM((SEGS, 8, ROWS, 256), f32),
            pltpu.VMEM((8, SEGS * MINE, 256), f32),
            dma((6,)), dma((SEGS,)), dma((SEGS,)), dma((SEGS,)), dma((SEGS,)),
            dma((OWNERS,)), dma((OWNERS,)), dma((16,)), dma((16,)), pltpu.SemaphoreType.REGULAR((16,)),
        ],
        compiler_params=pltpu.CompilerParams(
            collective_id=0, has_side_effects=True, vmem_limit_bytes=60 * 2**20
        ),
        name="correlate",
    )(source_channels, valid_mask.reshape(1, ROWS), record, jnp.asarray(small), jnp.asarray(forward), jnp.asarray(inverse))


def solution(mesh):
    placed = (P("recv", "tm"), P(), P("recv", "tm"))
    return jax.shard_map(
        local, mesh=mesh, in_specs=placed, out_specs=P("tm", "recv", None), check_vma=False
    )
```

```python
import functools

import jax
import jax.numpy as jnp
import numpy as np
from jax import lax
from jax.experimental import pallas as pl
from jax.experimental.pallas import tpu as pltpu
from jax.sharding import PartitionSpec as P

SEGLEN = 2048
NF = 1024
LAGS = 256
SMOOTH = 64
NSRC = 16
SEGS = 4
ROWS = 16
HALF = 1024
LANES = 128
OWNERS = 8
PLANES = 8
COLS = 4
MINE = 4
MESH = pl.DeviceIdType.MESH


def split_bf16(table):
    bf16 = jnp.dtype(jnp.bfloat16)
    high = table.astype(bf16)
    low = (table - high.astype(np.float64)).astype(bf16)
    return high, low


@functools.cache
def tables():
    m = np.arange(16)[:, None]
    lane = np.arange(LANES)[None, :]
    taper = 0.5 - 0.5 * np.cos(2 * np.pi * (m * 128 + lane) / SEGLEN)
    twist = 2 * np.pi * m * lane / SEGLEN
    j = np.arange(8)[:, None]
    freq = j + 8 * (lane // 64) + 16 * (lane % 64)
    counts = np.minimum(freq + SMOOTH, NF - 1) - np.maximum(freq - SMOOTH, 0) + 1
    small = np.concatenate([taper, np.cos(twist), np.sin(twist), 1.0 / counts]).astype(np.float32)

    angle = 2 * np.pi * (np.arange(128)[:, None] * np.arange(64)[None, :] % 128) / 128
    forward = np.zeros((4, 128, 4, 64))
    for h in range(2):
        forward[2 * h, :, h] = np.cos(angle)
        forward[2 * h + 1, :, h] = np.sin(angle)
        forward[2 * h, :, 2 + h] = -np.sin(angle)
        forward[2 * h + 1, :, 2 + h] = np.cos(angle)
    forward = forward.reshape(512, 256)

    lag = np.arange(LAGS)[None, None, :] - LAGS // 2
    turn = 2 * np.pi * (freq[:, :, None] * lag % SEGLEN) / SEGLEN
    factor = np.where(freq == 0, 1.0, 2.0)[:, :, None] / SEGLEN
    inverse = np.stack([factor * np.cos(turn), -factor * np.sin(turn)], axis=1).reshape(2 * NF, LAGS)
    return small, np.stack(split_bf16(forward)), np.stack(split_bf16(inverse))


def halves(x):
    high = x.astype(jnp.bfloat16)
    low = (x - high.astype(jnp.float32)).astype(jnp.bfloat16)
    return high, low


def dot3(high, low, tab_high, tab_low):
    dot = functools.partial(jnp.dot, preferred_element_type=jnp.float32)
    return dot(high, tab_high) + dot(low, tab_high) + dot(high, tab_low)


def real_dft16(x):
    r2 = np.float32(np.sqrt(0.5))
    c1 = np.float32(np.cos(np.pi / 8))
    s1 = np.float32(np.sin(np.pi / 8))
    a = [x[m] + x[m + 8] for m in range(8)]
    b = [x[m] - x[m + 8] for m in range(8)]
    a2 = [a[m] + a[m + 4] for m in range(4)]
    b2 = [a[m] - a[m + 4] for m in range(4)]
    even, odd = a2[0] + a2[2], a2[1] + a2[3]
    out = [None] * 9
    out[0] = (even + odd, None)
    out[8] = (even - odd, None)
    out[4] = (a2[0] - a2[2], a2[3] - a2[1])
    diff, total = r2 * (b2[1] - b2[3]), r2 * (b2[1] + b2[3])
    out[2] = (b2[0] + diff, -(b2[2] + total))
    out[6] = (b2[0] - diff, b2[2] - total)
    u1, u2, u3 = b[1] - b[7], r2 * (b[2] - b[6]), b[3] - b[5]
    v1, v2, v3 = b[1] + b[7], r2 * (b[2] + b[6]), b[3] + b[5]
    up, um = b[0] + u2, b[0] - u2
    vp, vm = v2 + b[4], v2 - b[4]
    p, q = c1 * u1 + s1 * u3, s1 * u1 - c1 * u3
    out[1] = (up + p, -(s1 * v1 + c1 * v3 + vp))
    out[7] = (up - p, -(s1 * v1 + c1 * v3 - vp))
    out[3] = (um + q, -(c1 * v1 - s1 * v3 + vm))
    out[5] = (um - q, -(c1 * v1 - s1 * v3 - vm))
    return out


def whitened(x, small, forward):
    total = x[0]
    for m in range(1, 16):
        total = total + x[m]
    mean = jnp.sum(total, axis=1, keepdims=True) * (1.0 / SEGLEN)
    tapered = [(x[m] - mean) * small[m : m + 1, :] for m in range(16)]
    base = real_dft16(tapered)
    mid = []
    for f in range(16):
        re, im = base[min(f, 16 - f)]
        if im is not None and f > 8:
            im = -im
        cos, sin = small[16 + f : 17 + f, :], small[32 + f : 33 + f, :]
        if f == 0:
            mid.append((re, jnp.zeros_like(re)))
        elif im is None:
            mid.append((re * cos, -(re * sin)))
        else:
            mid.append((re * cos + im * sin, im * cos - re * sin))
    highs, lows = [], []
    for j in range(8):
        parts = [halves(v) for v in (*mid[j], *mid[j + 8])]
        highs.append(jnp.concatenate([p[0] for p in parts], axis=1))
        lows.append(jnp.concatenate([p[1] for p in parts], axis=1))
    spec = dot3(jnp.concatenate(highs, axis=0), jnp.concatenate(lows, axis=0), forward[0], forward[1])
    rows = x[0].shape[0]
    re = [spec[j * rows : (j + 1) * rows, :LANES] for j in range(8)]
    im = [spec[j * rows : (j + 1) * rows, LANES:] for j in range(8)]
    power = [re[j] * re[j] + im[j] * im[j] for j in range(8)]

    lane = lax.broadcasted_iota(jnp.int32, power[0].shape, 1)
    bin_g = lane % 64
    lower = lane < 64
    zero = jnp.zeros_like(power[0])
    ahead, behind = [power[0]], [power[7]]
    for j in range(1, 8):
        ahead.append(ahead[-1] + power[j])
        behind.append(behind[-1] + power[7 - j])
    behind.reverse()
    other = pltpu.roll(ahead[7], 64, 1)
    lower_total = jnp.where(lower, zero, other)
    upper_total = jnp.where(lower, other, zero)
    all_f = jnp.where(lower, ahead[7] + other, zero)
    three = all_f + pltpu.roll(all_f, 1, 1) + pltpu.roll(all_f, 2, 1)
    seven = jnp.where(lower, pltpu.roll(three, 125, 1) + all_f + pltpu.roll(three, 1, 1), zero)
    seven = seven + pltpu.roll(seven, 64, 1)
    out_re, out_im = [], []
    for j in range(8):
        above = jnp.where(bin_g < 60, pltpu.roll(ahead[j] + lower_total, 124, 1), zero)
        below = jnp.where(bin_g >= 4, pltpu.roll(behind[j] + upper_total, 4, 1), zero)
        smoothed = (seven + above + below) * small[48 + j : 49 + j, :]
        scale = lax.rsqrt(smoothed + 1e-06)
        out_re.append(re[j] * scale)
        out_im.append(im[j] * scale)
    return out_re, out_im


def kernel(
    chan_hbm, mask_hbm, rec_hbm, small_hbm, fwd_hbm, inv_hbm, out_ref,
    chan_ref, mask_ref, rec_ref, small_ref, fwd_ref, inv_ref, all_ref, val_ref, vsend_ref, send1_ref, recv1_ref, send2_ref, recv2_ref,
    white_ref, src_ref,
    tab_sem, rec_ssem, rec_rsem, val_ssem, val_rsem, ssem1, rsem1, ssem2, rsem2, ready_sem,
):
    r = lax.axis_index("recv")
    t = lax.axis_index("tm")
    x, yh, z = r % COLS, (r // COLS) % 4, r // 16
    cand = r % OWNERS
    group = r // OWNERS
    dest = z // 2

    loads = [
        pltpu.make_async_copy(src, dst, tab_sem.at[n])
        for n, (src, dst) in enumerate(
            (
                (rec_hbm, rec_ref),
                (chan_hbm, chan_ref),
                (mask_hbm, mask_ref),
                (small_hbm, small_ref),
                (fwd_hbm, fwd_ref),
                (inv_hbm, inv_ref),
            )
        )
    ]
    for load in loads:
        load.start()

    barrier = pltpu.get_barrier_semaphore()

    def greet(recv, tm):
        pl.semaphore_signal(barrier, inc=1, device_id={"recv": recv, "tm": tm}, device_id_type=MESH)

    rows = (yh, 3 - yh)
    for d in range(1, OWNERS):
        greet(group * OWNERS + (cand + d) % OWNERS, t)
    for d in range(1, SEGS):
        greet(r, (t + d) % SEGS)

    @pl.when(t == dest)
    def _():
        for b in range(SEGS):
            greet(z * 16 + rows[1] * COLS + x, b)

    for p in range(2):

        @pl.when(2 * t + p > z)
        def _(p=p):
            for b in range(SEGS):
                for row in rows:
                    greet((2 * t + p) * 16 + row * COLS + x, b)

    for target in range(1, PLANES):

        @pl.when(target > z)
        def _(target=target):
            for row in rows:
                greet(target * 16 + row * COLS + x, dest)

    for load in loads[:3]:
        load.wait()
    rec = rec_ref[...]
    mask = jnp.broadcast_to(mask_ref[...].astype(jnp.float32), (ROWS, ROWS))
    square = (ROWS, ROWS)
    diagonal = lax.broadcasted_iota(jnp.int32, square, 0) == lax.broadcasted_iota(jnp.int32, square, 1)
    mask = jnp.sum(jnp.where(diagonal, mask, 0.0), axis=1, keepdims=True)
    valid = jnp.broadcast_to(mask, (ROWS, LANES))
    vsend_ref[...] = valid
    val_ref[t] = valid
    all_ref[t] = rec
    all_ref[SEGS] = jnp.zeros((ROWS, HALF), jnp.float32)

    index = jnp.clip(chan_ref[group] - r * ROWS, 0, ROWS - 1)
    picked = rec_ref[pl.ds(index, 1), :]
    for m in range(8):
        piece = picked[:, m * LANES : (m + 1) * LANES]
        send1_ref[pl.ds(m, 1), :] = piece
        recv1_ref[cand, pl.ds(m, 1), :] = piece
    piece = vsend_ref[pl.ds(index, 1), :]
    send1_ref[pl.ds(8, 1), :] = piece
    recv1_ref[cand, pl.ds(8, 1), :] = piece

    lower_holders = jnp.clip(z - 2 * t, 0, 2)
    pl.semaphore_wait(barrier, (OWNERS - 1) + (SEGS - 1) + 1 + 2 * z + 8 * lower_holders)

    for p in range(2):

        @pl.when(2 * t + p < z)
        def _(p=p):
            for b in range(SEGS):
                for flip, row in enumerate(rows):
                    pl.semaphore_signal(
                        ready_sem.at[2 * z + flip], inc=1,
                        device_id={"recv": (2 * t + p) * 16 + row * COLS + x, "tm": b}, device_id_type=MESH,
                    )

    sends = []
    for d in range(1, OWNERS):
        copy = pltpu.make_async_remote_copy(
            send1_ref, recv1_ref.at[cand], ssem1.at[d], rsem1.at[cand],
            device_id={"recv": group * OWNERS + (cand + d) % OWNERS, "tm": t}, device_id_type=MESH,
        )
        copy.start()
        sends.append(copy)
    for d in range(1, SEGS):
        to = {"recv": r, "tm": (t + d) % SEGS}
        copy = pltpu.make_async_remote_copy(
            rec_ref, all_ref.at[t], rec_ssem.at[d], rec_rsem.at[t], device_id=to, device_id_type=MESH
        )
        copy.start()
        sends.append(copy)
        copy = pltpu.make_async_remote_copy(
            vsend_ref, val_ref.at[t], val_ssem.at[d], val_rsem.at[t], device_id=to, device_id_type=MESH
        )
        copy.start()
        sends.append(copy)

    def arrived(buf, sem):
        pltpu.make_async_remote_copy(
            buf, buf, sem, sem, device_id={"recv": r, "tm": t}, device_id_type=MESH
        ).wait_recv()

    for d in range(1, OWNERS):
        slot = (cand + d) % OWNERS
        arrived(recv1_ref.at[slot], rsem1.at[slot])

    owner = jnp.clip((chan_ref[group] - group * (OWNERS * ROWS)) // ROWS, 0, OWNERS - 1)
    chosen = recv1_ref[owner]
    send2_ref[...] = chosen
    entry = t * MINE + (z % 2) * 2 + yh // 2

    @pl.when(t == dest)
    def _():
        recv2_ref[entry] = chosen

    def spread(target, flip):
        return pltpu.make_async_remote_copy(
            send2_ref, recv2_ref.at[entry], ssem2.at[2 * target + flip], rsem2.at[entry],
            device_id={"recv": target * 16 + rows[flip] * COLS + x, "tm": dest}, device_id_type=MESH,
        )

    for target in range(PLANES):
        pl.when(target <= z)(spread(target, 1).start)
        pl.when(jnp.logical_or(target < z, jnp.logical_and(target == z, t != dest)))(spread(target, 0).start)

    for d in range(1, SEGS):
        slot = (t + d) % SEGS
        arrived(all_ref.at[slot], rec_rsem.at[slot])
        arrived(val_ref.at[slot], val_rsem.at[slot])
    loads[3].wait()
    loads[4].wait()
    small = small_ref[...]

    @pl.loop(0, SEGS)
    def _(k):
        first, second = all_ref[k], all_ref[k + 1]
        xs = [first[:, m * LANES : (m + 1) * LANES] for m in range(8)]
        xs += [second[:, m * LANES : (m + 1) * LANES] for m in range(8)]
        re, im = whitened(xs, small, (fwd_ref[0], fwd_ref[1]))
        for j in range(8):
            white_ref[k, j, :, :LANES] = re[j]
            white_ref[k, j, :, LANES:] = im[j]

    for target in range(1, PLANES):

        @pl.when(target > z)
        def _(target=target):
            for flip in range(2):
                pl.semaphore_wait(ready_sem.at[2 * target + flip], 1)
                spread(target, flip).start()

    for copy in sends:
        copy.wait_send()

    for target in range(PLANES):
        spread(target, 1).wait_send()
        pl.when(jnp.logical_or(target != z, t != dest))(spread(target, 0).wait_send)

    for e in range(SEGS * MINE):
        b, p, h = e // MINE, (e % MINE) // 2, e % 2
        own = jnp.logical_and(jnp.logical_and(t == b, z == 2 * t + p), yh // 2 == h)

        @pl.when(jnp.logical_not(own))
        def _(e=e):
            arrived(recv2_ref.at[e], rsem2.at[e])

    none = jnp.zeros((MINE, LANES), jnp.float32)
    xs = [recv2_ref[:, m, :] for m in range(8)]
    xs += [jnp.concatenate([v[MINE:], none], axis=0) for v in xs]
    re, im = whitened(xs, small, (fwd_ref[0], fwd_ref[1]))
    for j in range(8):
        src_ref[j, :, :LANES] = re[j]
        src_ref[j, :, LANES:] = im[j]

    def cross(j, first):
        highs, lows = [], []
        for k in range(SEGS):
            rec_re, rec_im = white_ref[k, j, :, :LANES], white_ref[k, j, :, LANES:]
            for s in range(first, first + 2):
                src = src_ref[j, pl.ds(k * MINE + s, 1), :]
                src_re, src_im = src[:, :LANES], src[:, LANES:]
                parts = halves(src_re * rec_re + src_im * rec_im), halves(src_re * rec_im - src_im * rec_re)
                highs.append(jnp.concatenate([p[0] for p in parts], axis=1))
                lows.append(jnp.concatenate([p[1] for p in parts], axis=1))
        return jnp.concatenate(highs, axis=0), jnp.concatenate(lows, axis=0)

    loads[5].wait()
    for first in (0, 2):
        lag = None
        for j in range(8):
            high, low = cross(j, first)
            block = pl.ds(j * 256, 256)
            term = dot3(high, low, inv_ref[0, block, :], inv_ref[1, block, :])
            lag = term if lag is None else lag + term
        power = jnp.sum(lag * lag, axis=1, keepdims=True) * (1.0 / LAGS)
        scale = lax.rsqrt(power + 1e-06)
        for s in range(2):
            stack = None
            for k in range(SEGS):
                row = (2 * k + s) * ROWS
                weight = val_ref[k] * recv2_ref[k * MINE + first + s, pl.ds(8, 1), :]
                term = lag[row : row + ROWS] * (scale[row : row + ROWS] * weight[:, :1])
                stack = term if stack is None else stack + term
            out_ref[first + s] = stack


def local(record, source_channels, valid_mask):
    small, forward, inverse = tables()
    f32, bf16 = jnp.float32, jnp.bfloat16
    vmem = pl.BlockSpec(memory_space=pltpu.VMEM)
    hbm = pl.BlockSpec(memory_space=pltpu.HBM)
    dma = pltpu.SemaphoreType.DMA
    return pl.pallas_call(
        kernel,
        out_shape=pltpu.VMEM((MINE, ROWS, LAGS), f32),
        in_specs=[hbm] * 6,
        out_specs=vmem,
        scratch_shapes=[
            pltpu.SMEM((NSRC,), jnp.int32),
            pltpu.VMEM((1, ROWS), jnp.int32),
            pltpu.VMEM((ROWS, HALF), f32),
            pltpu.VMEM(small.shape, f32),
            pltpu.VMEM(forward.shape, bf16),
            pltpu.VMEM(inverse.shape, bf16),
            pltpu.VMEM((SEGS + 1, ROWS, HALF), f32),
            pltpu.VMEM((SEGS, ROWS, LANES), f32),
            pltpu.VMEM((ROWS, LANES), f32),
            pltpu.VMEM((9, LANES), f32),
            pltpu.VMEM((OWNERS, 9, LANES), f32),
            pltpu.VMEM((9, LANES), f32),
            pltpu.VMEM((SEGS * MINE, 9, LANES), f32),
            pltpu.VMEM((SEGS, 8, ROWS, 256), f32),
            pltpu.VMEM((8, SEGS * MINE, 256), f32),
            dma((6,)), dma((SEGS,)), dma((SEGS,)), dma((SEGS,)), dma((SEGS,)),
            dma((OWNERS,)), dma((OWNERS,)), dma((16,)), dma((16,)), pltpu.SemaphoreType.REGULAR((16,)),
        ],
        compiler_params=pltpu.CompilerParams(
            collective_id=0, has_side_effects=True, vmem_limit_bytes=60 * 2**20
        ),
        name="correlate",
    )(source_channels, valid_mask.reshape(1, ROWS), record, jnp.asarray(small), jnp.asarray(forward), jnp.asarray(inverse))


def solution(mesh):
    placed = (P("recv", "tm"), P(), P("recv", "tm"))
    return jax.shard_map(
        local, mesh=mesh, in_specs=placed, out_specs=P("tm", "recv", None), check_vma=False
    )
```

```python
import functools

import jax
import jax.numpy as jnp
import numpy as np
from jax import lax
from jax.experimental import pallas as pl
from jax.experimental.pallas import tpu as pltpu
from jax.sharding import PartitionSpec as P

SEGLEN = 2048
NF = 1024
LAGS = 256
SMOOTH = 64
NSRC = 16
SEGS = 4
ROWS = 16
HALF = 1024
LANES = 128
OWNERS = 8
PLANES = 8
COLS = 4
MINE = 4
MESH = pl.DeviceIdType.MESH


def split_bf16(table):
    bf16 = jnp.dtype(jnp.bfloat16)
    high = table.astype(bf16)
    low = (table - high.astype(np.float64)).astype(bf16)
    return high, low


@functools.cache
def tables():
    m = np.arange(16)[:, None]
    lane = np.arange(LANES)[None, :]
    taper = 0.5 - 0.5 * np.cos(2 * np.pi * (m * 128 + lane) / SEGLEN)
    twist = 2 * np.pi * m * lane / SEGLEN
    j = np.arange(8)[:, None]
    freq = j + 8 * (lane // 64) + 16 * (lane % 64)
    counts = np.minimum(freq + SMOOTH, NF - 1) - np.maximum(freq - SMOOTH, 0) + 1
    small = np.concatenate([taper, np.cos(twist), np.sin(twist), 1.0 / counts]).astype(np.float32)

    angle = 2 * np.pi * (np.arange(128)[:, None] * np.arange(64)[None, :] % 128) / 128
    forward = np.zeros((4, 128, 4, 64))
    for h in range(2):
        forward[2 * h, :, h] = np.cos(angle)
        forward[2 * h + 1, :, h] = np.sin(angle)
        forward[2 * h, :, 2 + h] = -np.sin(angle)
        forward[2 * h + 1, :, 2 + h] = np.cos(angle)
    forward = forward.reshape(512, 256)

    lag = np.arange(LAGS)[None, None, :] - LAGS // 2
    turn = 2 * np.pi * (freq[:, :, None] * lag % SEGLEN) / SEGLEN
    factor = np.where(freq == 0, 1.0, 2.0)[:, :, None] / SEGLEN
    inverse = np.stack([factor * np.cos(turn), -factor * np.sin(turn)], axis=1).reshape(2 * NF, LAGS)
    return small, np.stack(split_bf16(forward)), np.stack(split_bf16(inverse))


def halves(x):
    high = x.astype(jnp.bfloat16)
    low = (x - high.astype(jnp.float32)).astype(jnp.bfloat16)
    return high, low


def dot3(high, low, tab_high, tab_low):
    dot = functools.partial(jnp.dot, preferred_element_type=jnp.float32)
    return dot(high, tab_high) + dot(low, tab_high) + dot(high, tab_low)


def real_dft16(x):
    r2 = np.float32(np.sqrt(0.5))
    c1 = np.float32(np.cos(np.pi / 8))
    s1 = np.float32(np.sin(np.pi / 8))
    a = [x[m] + x[m + 8] for m in range(8)]
    b = [x[m] - x[m + 8] for m in range(8)]
    a2 = [a[m] + a[m + 4] for m in range(4)]
    b2 = [a[m] - a[m + 4] for m in range(4)]
    even, odd = a2[0] + a2[2], a2[1] + a2[3]
    out = [None] * 9
    out[0] = (even + odd, None)
    out[8] = (even - odd, None)
    out[4] = (a2[0] - a2[2], a2[3] - a2[1])
    diff, total = r2 * (b2[1] - b2[3]), r2 * (b2[1] + b2[3])
    out[2] = (b2[0] + diff, -(b2[2] + total))
    out[6] = (b2[0] - diff, b2[2] - total)
    u1, u2, u3 = b[1] - b[7], r2 * (b[2] - b[6]), b[3] - b[5]
    v1, v2, v3 = b[1] + b[7], r2 * (b[2] + b[6]), b[3] + b[5]
    up, um = b[0] + u2, b[0] - u2
    vp, vm = v2 + b[4], v2 - b[4]
    p, q = c1 * u1 + s1 * u3, s1 * u1 - c1 * u3
    out[1] = (up + p, -(s1 * v1 + c1 * v3 + vp))
    out[7] = (up - p, -(s1 * v1 + c1 * v3 - vp))
    out[3] = (um + q, -(c1 * v1 - s1 * v3 + vm))
    out[5] = (um - q, -(c1 * v1 - s1 * v3 - vm))
    return out


def whitened(x, small, forward):
    total = x[0]
    for m in range(1, 16):
        total = total + x[m]
    mean = jnp.sum(total, axis=1, keepdims=True) * (1.0 / SEGLEN)
    tapered = [(x[m] - mean) * small[m : m + 1, :] for m in range(16)]
    base = real_dft16(tapered)
    mid = []
    for f in range(16):
        re, im = base[min(f, 16 - f)]
        if im is not None and f > 8:
            im = -im
        cos, sin = small[16 + f : 17 + f, :], small[32 + f : 33 + f, :]
        if f == 0:
            mid.append((re, jnp.zeros_like(re)))
        elif im is None:
            mid.append((re * cos, -(re * sin)))
        else:
            mid.append((re * cos + im * sin, im * cos - re * sin))
    highs, lows = [], []
    for j in range(8):
        parts = [halves(v) for v in (*mid[j], *mid[j + 8])]
        highs.append(jnp.concatenate([p[0] for p in parts], axis=1))
        lows.append(jnp.concatenate([p[1] for p in parts], axis=1))
    spec = dot3(jnp.concatenate(highs, axis=0), jnp.concatenate(lows, axis=0), forward[0], forward[1])
    rows = x[0].shape[0]
    re = [spec[j * rows : (j + 1) * rows, :LANES] for j in range(8)]
    im = [spec[j * rows : (j + 1) * rows, LANES:] for j in range(8)]
    power = [re[j] * re[j] + im[j] * im[j] for j in range(8)]

    lane = lax.broadcasted_iota(jnp.int32, power[0].shape, 1)
    bin_g = lane % 64
    lower = lane < 64
    zero = jnp.zeros_like(power[0])
    ahead, behind = [power[0]], [power[7]]
    for j in range(1, 8):
        ahead.append(ahead[-1] + power[j])
        behind.append(behind[-1] + power[7 - j])
    behind.reverse()
    other = pltpu.roll(ahead[7], 64, 1)
    lower_total = jnp.where(lower, zero, other)
    upper_total = jnp.where(lower, other, zero)
    all_f = jnp.where(lower, ahead[7] + other, zero)
    three = all_f + pltpu.roll(all_f, 1, 1) + pltpu.roll(all_f, 2, 1)
    seven = jnp.where(lower, pltpu.roll(three, 125, 1) + all_f + pltpu.roll(three, 1, 1), zero)
    seven = seven + pltpu.roll(seven, 64, 1)
    out_re, out_im = [], []
    for j in range(8):
        above = jnp.where(bin_g < 60, pltpu.roll(ahead[j] + lower_total, 124, 1), zero)
        below = jnp.where(bin_g >= 4, pltpu.roll(behind[j] + upper_total, 4, 1), zero)
        smoothed = (seven + above + below) * small[48 + j : 49 + j, :]
        scale = lax.rsqrt(smoothed + 1e-06)
        out_re.append(re[j] * scale)
        out_im.append(im[j] * scale)
    return out_re, out_im


def kernel(
    chan_hbm, mask_hbm, rec_hbm, small_hbm, fwd_hbm, inv_hbm, out_ref,
    chan_ref, mask_ref, rec_ref, small_ref, fwd_ref, inv_ref, all_ref, val_ref, vsend_ref, send1_ref, recv1_ref, send2_ref, recv2_ref,
    white_ref, src_ref,
    tab_sem, rec_ssem, rec_rsem, val_ssem, val_rsem, ssem1, rsem1, ssem2, rsem2, ready_sem,
):
    r = lax.axis_index("recv")
    t = lax.axis_index("tm")
    x, yh, z = r % COLS, (r // COLS) % 4, r // 16
    cand = r % OWNERS
    group = r // OWNERS
    dest = z // 2

    loads = [
        pltpu.make_async_copy(src, dst, tab_sem.at[n])
        for n, (src, dst) in enumerate(
            (
                (rec_hbm, rec_ref),
                (chan_hbm, chan_ref),
                (mask_hbm, mask_ref),
                (small_hbm, small_ref),
                (fwd_hbm, fwd_ref),
                (inv_hbm, inv_ref),
            )
        )
    ]
    for load in loads:
        load.start()

    barrier = pltpu.get_barrier_semaphore()

    def greet(recv, tm):
        pl.semaphore_signal(barrier, inc=1, device_id={"recv": recv, "tm": tm}, device_id_type=MESH)

    rows = (yh, 3 - yh)
    for d in range(1, OWNERS):
        greet(group * OWNERS + (cand + d) % OWNERS, t)
    for d in range(1, SEGS):
        greet(r, (t + d) % SEGS)

    @pl.when(t == dest)
    def _():
        for b in range(SEGS):
            greet(z * 16 + rows[1] * COLS + x, b)

    for p in range(2):

        @pl.when(2 * t + p > z)
        def _(p=p):
            for b in range(SEGS):
                for row in rows:
                    greet((2 * t + p) * 16 + row * COLS + x, b)

    for target in range(1, PLANES):

        @pl.when(target > z)
        def _(target=target):
            for row in rows:
                greet(target * 16 + row * COLS + x, dest)

    for load in loads[:3]:
        load.wait()
    rec = rec_ref[...]
    mask = jnp.broadcast_to(mask_ref[...].astype(jnp.float32), (ROWS, ROWS))
    square = (ROWS, ROWS)
    diagonal = lax.broadcasted_iota(jnp.int32, square, 0) == lax.broadcasted_iota(jnp.int32, square, 1)
    mask = jnp.sum(jnp.where(diagonal, mask, 0.0), axis=1, keepdims=True)
    valid = jnp.broadcast_to(mask, (ROWS, LANES))
    vsend_ref[...] = valid
    val_ref[t] = valid
    all_ref[t] = rec
    all_ref[SEGS] = jnp.zeros((ROWS, HALF), jnp.float32)

    index = jnp.clip(chan_ref[group] - r * ROWS, 0, ROWS - 1)
    picked = rec_ref[pl.ds(index, 1), :]
    for m in range(8):
        piece = picked[:, m * LANES : (m + 1) * LANES]
        send1_ref[pl.ds(m, 1), :] = piece
        recv1_ref[cand, pl.ds(m, 1), :] = piece
    piece = vsend_ref[pl.ds(index, 1), :]
    send1_ref[pl.ds(8, 1), :] = piece
    recv1_ref[cand, pl.ds(8, 1), :] = piece

    lower_holders = jnp.clip(z - 2 * t, 0, 2)
    pl.semaphore_wait(barrier, (OWNERS - 1) + (SEGS - 1) + 1 + 2 * z + 8 * lower_holders)

    for p in range(2):

        @pl.when(2 * t + p < z)
        def _(p=p):
            for b in range(SEGS):
                for flip, row in enumerate(rows):
                    pl.semaphore_signal(
                        ready_sem.at[2 * z + flip], inc=1,
                        device_id={"recv": (2 * t + p) * 16 + row * COLS + x, "tm": b}, device_id_type=MESH,
                    )

    sends = []
    for d in range(1, OWNERS):
        copy = pltpu.make_async_remote_copy(
            send1_ref, recv1_ref.at[cand], ssem1.at[d], rsem1.at[cand],
            device_id={"recv": group * OWNERS + (cand + d) % OWNERS, "tm": t}, device_id_type=MESH,
        )
        copy.start()
        sends.append(copy)
    def arrived(buf, sem):
        pltpu.make_async_remote_copy(
            buf, buf, sem, sem, device_id={"recv": r, "tm": t}, device_id_type=MESH
        ).wait_recv()

    for d in range(1, OWNERS):
        slot = (cand + d) % OWNERS
        arrived(recv1_ref.at[slot], rsem1.at[slot])

    owner = jnp.clip((chan_ref[group] - group * (OWNERS * ROWS)) // ROWS, 0, OWNERS - 1)
    chosen = recv1_ref[owner]
    send2_ref[...] = chosen
    entry = t * MINE + (z % 2) * 2 + yh // 2

    @pl.when(t == dest)
    def _():
        recv2_ref[entry] = chosen

    def spread(target, flip):
        return pltpu.make_async_remote_copy(
            send2_ref, recv2_ref.at[entry], ssem2.at[2 * target + flip], rsem2.at[entry],
            device_id={"recv": target * 16 + rows[flip] * COLS + x, "tm": dest}, device_id_type=MESH,
        )

    for target in range(PLANES):
        pl.when(target <= z)(spread(target, 1).start)
        pl.when(jnp.logical_or(target < z, jnp.logical_and(target == z, t != dest)))(spread(target, 0).start)

    for d in range(1, SEGS):
        to = {"recv": r, "tm": (t + d) % SEGS}
        copy = pltpu.make_async_remote_copy(
            rec_ref, all_ref.at[t], rec_ssem.at[d], rec_rsem.at[t], device_id=to, device_id_type=MESH
        )
        copy.start()
        sends.append(copy)
        copy = pltpu.make_async_remote_copy(
            vsend_ref, val_ref.at[t], val_ssem.at[d], val_rsem.at[t], device_id=to, device_id_type=MESH
        )
        copy.start()
        sends.append(copy)

    for d in range(1, SEGS):
        slot = (t + d) % SEGS
        arrived(all_ref.at[slot], rec_rsem.at[slot])
        arrived(val_ref.at[slot], val_rsem.at[slot])
    loads[3].wait()
    loads[4].wait()
    small = small_ref[...]

    @pl.loop(0, SEGS)
    def _(k):
        first, second = all_ref[k], all_ref[k + 1]
        xs = [first[:, m * LANES : (m + 1) * LANES] for m in range(8)]
        xs += [second[:, m * LANES : (m + 1) * LANES] for m in range(8)]
        re, im = whitened(xs, small, (fwd_ref[0], fwd_ref[1]))
        for j in range(8):
            white_ref[k, j, :, :LANES] = re[j]
            white_ref[k, j, :, LANES:] = im[j]

    for target in range(1, PLANES):

        @pl.when(target > z)
        def _(target=target):
            for flip in range(2):
                pl.semaphore_wait(ready_sem.at[2 * target + flip], 1)
                spread(target, flip).start()

    for copy in sends:
        copy.wait_send()

    for target in range(PLANES):
        spread(target, 1).wait_send()
        pl.when(jnp.logical_or(target != z, t != dest))(spread(target, 0).wait_send)

    for e in range(SEGS * MINE):
        b, p, h = e // MINE, (e % MINE) // 2, e % 2
        own = jnp.logical_and(jnp.logical_and(t == b, z == 2 * t + p), yh // 2 == h)

        @pl.when(jnp.logical_not(own))
        def _(e=e):
            arrived(recv2_ref.at[e], rsem2.at[e])

    none = jnp.zeros((MINE, LANES), jnp.float32)
    xs = [recv2_ref[:, m, :] for m in range(8)]
    xs += [jnp.concatenate([v[MINE:], none], axis=0) for v in xs]
    re, im = whitened(xs, small, (fwd_ref[0], fwd_ref[1]))
    for j in range(8):
        src_ref[j, :, :LANES] = re[j]
        src_ref[j, :, LANES:] = im[j]

    def cross(j, first):
        highs, lows = [], []
        for k in range(SEGS):
            rec_re, rec_im = white_ref[k, j, :, :LANES], white_ref[k, j, :, LANES:]
            for s in range(first, first + 2):
                src = src_ref[j, pl.ds(k * MINE + s, 1), :]
                src_re, src_im = src[:, :LANES], src[:, LANES:]
                parts = halves(src_re * rec_re + src_im * rec_im), halves(src_re * rec_im - src_im * rec_re)
                highs.append(jnp.concatenate([p[0] for p in parts], axis=1))
                lows.append(jnp.concatenate([p[1] for p in parts], axis=1))
        return jnp.concatenate(highs, axis=0), jnp.concatenate(lows, axis=0)

    loads[5].wait()
    for first in (0, 2):
        lag = None
        for j in range(8):
            high, low = cross(j, first)
            block = pl.ds(j * 256, 256)
            term = dot3(high, low, inv_ref[0, block, :], inv_ref[1, block, :])
            lag = term if lag is None else lag + term
        power = jnp.sum(lag * lag, axis=1, keepdims=True) * (1.0 / LAGS)
        scale = lax.rsqrt(power + 1e-06)
        for s in range(2):
            stack = None
            for k in range(SEGS):
                row = (2 * k + s) * ROWS
                weight = val_ref[k] * recv2_ref[k * MINE + first + s, pl.ds(8, 1), :]
                term = lag[row : row + ROWS] * (scale[row : row + ROWS] * weight[:, :1])
                stack = term if stack is None else stack + term
            out_ref[first + s] = stack


def local(record, source_channels, valid_mask):
    small, forward, inverse = tables()
    f32, bf16 = jnp.float32, jnp.bfloat16
    vmem = pl.BlockSpec(memory_space=pltpu.VMEM)
    hbm = pl.BlockSpec(memory_space=pltpu.HBM)
    dma = pltpu.SemaphoreType.DMA
    return pl.pallas_call(
        kernel,
        out_shape=pltpu.VMEM((MINE, ROWS, LAGS), f32),
        in_specs=[hbm] * 6,
        out_specs=vmem,
        scratch_shapes=[
            pltpu.SMEM((NSRC,), jnp.int32),
            pltpu.VMEM((1, ROWS), jnp.int32),
            pltpu.VMEM((ROWS, HALF), f32),
            pltpu.VMEM(small.shape, f32),
            pltpu.VMEM(forward.shape, bf16),
            pltpu.VMEM(inverse.shape, bf16),
            pltpu.VMEM((SEGS + 1, ROWS, HALF), f32),
            pltpu.VMEM((SEGS, ROWS, LANES), f32),
            pltpu.VMEM((ROWS, LANES), f32),
            pltpu.VMEM((9, LANES), f32),
            pltpu.VMEM((OWNERS, 9, LANES), f32),
            pltpu.VMEM((9, LANES), f32),
            pltpu.VMEM((SEGS * MINE, 9, LANES), f32),
            pltpu.VMEM((SEGS, 8, ROWS, 256), f32),
            pltpu.VMEM((8, SEGS * MINE, 256), f32),
            dma((6,)), dma((SEGS,)), dma((SEGS,)), dma((SEGS,)), dma((SEGS,)),
            dma((OWNERS,)), dma((OWNERS,)), dma((16,)), dma((16,)), pltpu.SemaphoreType.REGULAR((16,)),
        ],
        compiler_params=pltpu.CompilerParams(
            collective_id=0, has_side_effects=True, vmem_limit_bytes=60 * 2**20
        ),
        name="correlate",
    )(source_channels, valid_mask.reshape(1, ROWS), record, jnp.asarray(small), jnp.asarray(forward), jnp.asarray(inverse))


def solution(mesh):
    placed = (P("recv", "tm"), P(), P("recv", "tm"))
    return jax.shard_map(
        local, mesh=mesh, in_specs=placed, out_specs=P("tm", "recv", None), check_vma=False
    )
```

```python
import functools

import jax
import jax.numpy as jnp
import numpy as np
from jax import lax
from jax.experimental import pallas as pl
from jax.experimental.pallas import tpu as pltpu
from jax.sharding import PartitionSpec as P

SEGLEN = 2048
NF = 1024
LAGS = 256
SMOOTH = 64
NSRC = 16
SEGS = 4
ROWS = 16
HALF = 1024
LANES = 128
OWNERS = 8
PLANES = 8
COLS = 4
MINE = 4
MESH = pl.DeviceIdType.MESH


def split_bf16(table):
    bf16 = jnp.dtype(jnp.bfloat16)
    high = table.astype(bf16)
    low = (table - high.astype(np.float64)).astype(bf16)
    return high, low


@functools.cache
def tables():
    m = np.arange(16)[:, None]
    lane = np.arange(LANES)[None, :]
    taper = 0.5 - 0.5 * np.cos(2 * np.pi * (m * 128 + lane) / SEGLEN)
    twist = 2 * np.pi * m * lane / SEGLEN
    j = np.arange(8)[:, None]
    freq = j + 8 * (lane // 64) + 16 * (lane % 64)
    counts = np.minimum(freq + SMOOTH, NF - 1) - np.maximum(freq - SMOOTH, 0) + 1
    small = np.concatenate([taper, np.cos(twist), np.sin(twist), 1.0 / counts]).astype(np.float32)

    angle = 2 * np.pi * (np.arange(128)[:, None] * np.arange(64)[None, :] % 128) / 128
    forward = np.zeros((4, 128, 4, 64))
    for h in range(2):
        forward[2 * h, :, h] = np.cos(angle)
        forward[2 * h + 1, :, h] = np.sin(angle)
        forward[2 * h, :, 2 + h] = -np.sin(angle)
        forward[2 * h + 1, :, 2 + h] = np.cos(angle)
    forward = forward.reshape(512, 256)

    lag = np.arange(LAGS)[None, None, :] - LAGS // 2
    turn = 2 * np.pi * (freq[:, :, None] * lag % SEGLEN) / SEGLEN
    factor = np.where(freq == 0, 1.0, 2.0)[:, :, None] / SEGLEN
    inverse = np.stack([factor * np.cos(turn), -factor * np.sin(turn)], axis=1).reshape(2 * NF, LAGS)
    return small, np.stack(split_bf16(forward)), np.stack(split_bf16(inverse))


def halves(x):
    high = x.astype(jnp.bfloat16)
    low = (x - high.astype(jnp.float32)).astype(jnp.bfloat16)
    return high, low


def dot3(high, low, tab_high, tab_low):
    dot = functools.partial(jnp.dot, preferred_element_type=jnp.float32)
    return dot(high, tab_high) + dot(low, tab_high) + dot(high, tab_low)


def real_dft16(x):
    r2 = np.float32(np.sqrt(0.5))
    c1 = np.float32(np.cos(np.pi / 8))
    s1 = np.float32(np.sin(np.pi / 8))
    a = [x[m] + x[m + 8] for m in range(8)]
    b = [x[m] - x[m + 8] for m in range(8)]
    a2 = [a[m] + a[m + 4] for m in range(4)]
    b2 = [a[m] - a[m + 4] for m in range(4)]
    even, odd = a2[0] + a2[2], a2[1] + a2[3]
    out = [None] * 9
    out[0] = (even + odd, None)
    out[8] = (even - odd, None)
    out[4] = (a2[0] - a2[2], a2[3] - a2[1])
    diff, total = r2 * (b2[1] - b2[3]), r2 * (b2[1] + b2[3])
    out[2] = (b2[0] + diff, -(b2[2] + total))
    out[6] = (b2[0] - diff, b2[2] - total)
    u1, u2, u3 = b[1] - b[7], r2 * (b[2] - b[6]), b[3] - b[5]
    v1, v2, v3 = b[1] + b[7], r2 * (b[2] + b[6]), b[3] + b[5]
    up, um = b[0] + u2, b[0] - u2
    vp, vm = v2 + b[4], v2 - b[4]
    p, q = c1 * u1 + s1 * u3, s1 * u1 - c1 * u3
    out[1] = (up + p, -(s1 * v1 + c1 * v3 + vp))
    out[7] = (up - p, -(s1 * v1 + c1 * v3 - vp))
    out[3] = (um + q, -(c1 * v1 - s1 * v3 + vm))
    out[5] = (um - q, -(c1 * v1 - s1 * v3 - vm))
    return out


def whitened(x, small, forward):
    total = x[0]
    for m in range(1, 16):
        total = total + x[m]
    mean = jnp.sum(total, axis=1, keepdims=True) * (1.0 / SEGLEN)
    tapered = [(x[m] - mean) * small[m : m + 1, :] for m in range(16)]
    base = real_dft16(tapered)
    mid = []
    for f in range(16):
        re, im = base[min(f, 16 - f)]
        if im is not None and f > 8:
            im = -im
        cos, sin = small[16 + f : 17 + f, :], small[32 + f : 33 + f, :]
        if f == 0:
            mid.append((re, jnp.zeros_like(re)))
        elif im is None:
            mid.append((re * cos, -(re * sin)))
        else:
            mid.append((re * cos + im * sin, im * cos - re * sin))
    highs, lows = [], []
    for j in range(8):
        parts = [halves(v) for v in (*mid[j], *mid[j + 8])]
        highs.append(jnp.concatenate([p[0] for p in parts], axis=1))
        lows.append(jnp.concatenate([p[1] for p in parts], axis=1))
    spec = dot3(jnp.concatenate(highs, axis=0), jnp.concatenate(lows, axis=0), forward[0], forward[1])
    rows = x[0].shape[0]
    re = [spec[j * rows : (j + 1) * rows, :LANES] for j in range(8)]
    im = [spec[j * rows : (j + 1) * rows, LANES:] for j in range(8)]
    power = [re[j] * re[j] + im[j] * im[j] for j in range(8)]

    lane = lax.broadcasted_iota(jnp.int32, power[0].shape, 1)
    bin_g = lane % 64
    lower = lane < 64
    zero = jnp.zeros_like(power[0])
    ahead, behind = [power[0]], [power[7]]
    for j in range(1, 8):
        ahead.append(ahead[-1] + power[j])
        behind.append(behind[-1] + power[7 - j])
    behind.reverse()
    other = pltpu.roll(ahead[7], 64, 1)
    lower_total = jnp.where(lower, zero, other)
    upper_total = jnp.where(lower, other, zero)
    all_f = jnp.where(lower, ahead[7] + other, zero)
    three = all_f + pltpu.roll(all_f, 1, 1) + pltpu.roll(all_f, 2, 1)
    seven = jnp.where(lower, pltpu.roll(three, 125, 1) + all_f + pltpu.roll(three, 1, 1), zero)
    seven = seven + pltpu.roll(seven, 64, 1)
    out_re, out_im = [], []
    for j in range(8):
        above = jnp.where(bin_g < 60, pltpu.roll(ahead[j] + lower_total, 124, 1), zero)
        below = jnp.where(bin_g >= 4, pltpu.roll(behind[j] + upper_total, 4, 1), zero)
        smoothed = (seven + above + below) * small[48 + j : 49 + j, :]
        scale = lax.rsqrt(smoothed + 1e-06)
        out_re.append(re[j] * scale)
        out_im.append(im[j] * scale)
    return out_re, out_im


def kernel(
    chan_hbm, mask_hbm, rec_hbm, small_hbm, fwd_hbm, inv_hbm, out_ref,
    chan_ref, mask_ref, rec_ref, small_ref, fwd_ref, inv_ref, all_ref, val_ref, vsend_ref, send1_ref, recv1_ref, send2_ref, recv2_ref,
    white_ref, src_ref,
    tab_sem, rec_ssem, rec_rsem, val_ssem, val_rsem, ssem1, rsem1, ssem2, rsem2, ready_sem,
):
    r = lax.axis_index("recv")
    t = lax.axis_index("tm")
    x, yh, z = r % COLS, (r // COLS) % 4, r // 16
    cand = r % OWNERS
    group = r // OWNERS
    dest = z // 2

    loads = [
        pltpu.make_async_copy(src, dst, tab_sem.at[n])
        for n, (src, dst) in enumerate(
            (
                (rec_hbm, rec_ref),
                (chan_hbm, chan_ref),
                (mask_hbm, mask_ref),
                (small_hbm, small_ref),
                (fwd_hbm, fwd_ref),
                (inv_hbm, inv_ref),
            )
        )
    ]
    for load in loads:
        load.start()

    barrier = pltpu.get_barrier_semaphore()

    def greet(recv, tm):
        pl.semaphore_signal(barrier, inc=1, device_id={"recv": recv, "tm": tm}, device_id_type=MESH)

    rows = (yh, 3 - yh)
    far_first = (6, 5, 7, 2, 4, 1, 3)
    for d in far_first:
        greet(group * OWNERS + (cand + d) % OWNERS, t)
    for d in range(1, SEGS):
        greet(r, (t + d) % SEGS)

    @pl.when(t == dest)
    def _():
        for b in range(SEGS):
            greet(z * 16 + rows[1] * COLS + x, b)

    for p in range(2):

        @pl.when(2 * t + p > z)
        def _(p=p):
            for b in range(SEGS):
                for row in rows:
                    greet((2 * t + p) * 16 + row * COLS + x, b)

    for target in range(1, PLANES):

        @pl.when(target > z)
        def _(target=target):
            for row in rows:
                greet(target * 16 + row * COLS + x, dest)

    for load in loads[:3]:
        load.wait()
    rec = rec_ref[...]
    mask = jnp.broadcast_to(mask_ref[...].astype(jnp.float32), (ROWS, ROWS))
    square = (ROWS, ROWS)
    diagonal = lax.broadcasted_iota(jnp.int32, square, 0) == lax.broadcasted_iota(jnp.int32, square, 1)
    mask = jnp.sum(jnp.where(diagonal, mask, 0.0), axis=1, keepdims=True)
    valid = jnp.broadcast_to(mask, (ROWS, LANES))
    vsend_ref[...] = valid
    val_ref[t] = valid
    all_ref[t] = rec
    all_ref[SEGS] = jnp.zeros((ROWS, HALF), jnp.float32)

    index = jnp.clip(chan_ref[group] - r * ROWS, 0, ROWS - 1)
    picked = rec_ref[pl.ds(index, 1), :]
    for m in range(8):
        piece = picked[:, m * LANES : (m + 1) * LANES]
        send1_ref[pl.ds(m, 1), :] = piece
        recv1_ref[cand, pl.ds(m, 1), :] = piece
    piece = vsend_ref[pl.ds(index, 1), :]
    send1_ref[pl.ds(8, 1), :] = piece
    recv1_ref[cand, pl.ds(8, 1), :] = piece

    lower_holders = jnp.clip(z - 2 * t, 0, 2)
    pl.semaphore_wait(barrier, (OWNERS - 1) + (SEGS - 1) + 1 + 2 * z + 8 * lower_holders)

    for p in range(2):

        @pl.when(2 * t + p < z)
        def _(p=p):
            for b in range(SEGS):
                for flip, row in enumerate(rows):
                    pl.semaphore_signal(
                        ready_sem.at[2 * z + flip], inc=1,
                        device_id={"recv": (2 * t + p) * 16 + row * COLS + x, "tm": b}, device_id_type=MESH,
                    )

    sends = []
    for d in far_first:
        copy = pltpu.make_async_remote_copy(
            send1_ref, recv1_ref.at[cand], ssem1.at[d], rsem1.at[cand],
            device_id={"recv": group * OWNERS + (cand + d) % OWNERS, "tm": t}, device_id_type=MESH,
        )
        copy.start()
        sends.append(copy)
    def arrived(buf, sem):
        pltpu.make_async_remote_copy(
            buf, buf, sem, sem, device_id={"recv": r, "tm": t}, device_id_type=MESH
        ).wait_recv()

    for d in range(1, OWNERS):
        slot = (cand + d) % OWNERS
        arrived(recv1_ref.at[slot], rsem1.at[slot])

    owner = jnp.clip((chan_ref[group] - group * (OWNERS * ROWS)) // ROWS, 0, OWNERS - 1)
    chosen = recv1_ref[owner]
    send2_ref[...] = chosen
    entry = t * MINE + (z % 2) * 2 + yh // 2

    @pl.when(t == dest)
    def _():
        recv2_ref[entry] = chosen

    def spread(target, flip):
        return pltpu.make_async_remote_copy(
            send2_ref, recv2_ref.at[entry], ssem2.at[2 * target + flip], rsem2.at[entry],
            device_id={"recv": target * 16 + rows[flip] * COLS + x, "tm": dest}, device_id_type=MESH,
        )

    for target in range(PLANES):
        pl.when(target <= z)(spread(target, 1).start)
        pl.when(jnp.logical_or(target < z, jnp.logical_and(target == z, t != dest)))(spread(target, 0).start)

    for d in range(1, SEGS):
        to = {"recv": r, "tm": (t + d) % SEGS}
        copy = pltpu.make_async_remote_copy(
            rec_ref, all_ref.at[t], rec_ssem.at[d], rec_rsem.at[t], device_id=to, device_id_type=MESH
        )
        copy.start()
        sends.append(copy)
        copy = pltpu.make_async_remote_copy(
            vsend_ref, val_ref.at[t], val_ssem.at[d], val_rsem.at[t], device_id=to, device_id_type=MESH
        )
        copy.start()
        sends.append(copy)

    for d in range(1, SEGS):
        slot = (t + d) % SEGS
        arrived(all_ref.at[slot], rec_rsem.at[slot])
        arrived(val_ref.at[slot], val_rsem.at[slot])
    loads[3].wait()
    loads[4].wait()
    small = small_ref[...]

    @pl.loop(0, SEGS)
    def _(k):
        first, second = all_ref[k], all_ref[k + 1]
        xs = [first[:, m * LANES : (m + 1) * LANES] for m in range(8)]
        xs += [second[:, m * LANES : (m + 1) * LANES] for m in range(8)]
        re, im = whitened(xs, small, (fwd_ref[0], fwd_ref[1]))
        for j in range(8):
            white_ref[k, j, :, :LANES] = re[j]
            white_ref[k, j, :, LANES:] = im[j]

    for target in range(1, PLANES):

        @pl.when(target > z)
        def _(target=target):
            for flip in range(2):
                pl.semaphore_wait(ready_sem.at[2 * target + flip], 1)
                spread(target, flip).start()

    for copy in sends:
        copy.wait_send()

    for target in range(PLANES):
        spread(target, 1).wait_send()
        pl.when(jnp.logical_or(target != z, t != dest))(spread(target, 0).wait_send)

    for e in range(SEGS * MINE):
        b, p, h = e // MINE, (e % MINE) // 2, e % 2
        own = jnp.logical_and(jnp.logical_and(t == b, z == 2 * t + p), yh // 2 == h)

        @pl.when(jnp.logical_not(own))
        def _(e=e):
            arrived(recv2_ref.at[e], rsem2.at[e])

    none = jnp.zeros((MINE, LANES), jnp.float32)
    xs = [recv2_ref[:, m, :] for m in range(8)]
    xs += [jnp.concatenate([v[MINE:], none], axis=0) for v in xs]
    re, im = whitened(xs, small, (fwd_ref[0], fwd_ref[1]))
    for j in range(8):
        src_ref[j, :, :LANES] = re[j]
        src_ref[j, :, LANES:] = im[j]

    def cross(j, first):
        highs, lows = [], []
        for k in range(SEGS):
            rec_re, rec_im = white_ref[k, j, :, :LANES], white_ref[k, j, :, LANES:]
            for s in range(first, first + 2):
                src = src_ref[j, pl.ds(k * MINE + s, 1), :]
                src_re, src_im = src[:, :LANES], src[:, LANES:]
                parts = halves(src_re * rec_re + src_im * rec_im), halves(src_re * rec_im - src_im * rec_re)
                highs.append(jnp.concatenate([p[0] for p in parts], axis=1))
                lows.append(jnp.concatenate([p[1] for p in parts], axis=1))
        return jnp.concatenate(highs, axis=0), jnp.concatenate(lows, axis=0)

    loads[5].wait()
    for first in (0, 2):
        lag = None
        for j in range(8):
            high, low = cross(j, first)
            block = pl.ds(j * 256, 256)
            term = dot3(high, low, inv_ref[0, block, :], inv_ref[1, block, :])
            lag = term if lag is None else lag + term
        power = jnp.sum(lag * lag, axis=1, keepdims=True) * (1.0 / LAGS)
        scale = lax.rsqrt(power + 1e-06)
        for s in range(2):
            stack = None
            for k in range(SEGS):
                row = (2 * k + s) * ROWS
                weight = val_ref[k] * recv2_ref[k * MINE + first + s, pl.ds(8, 1), :]
                term = lag[row : row + ROWS] * (scale[row : row + ROWS] * weight[:, :1])
                stack = term if stack is None else stack + term
            out_ref[first + s] = stack


def local(record, source_channels, valid_mask):
    small, forward, inverse = tables()
    f32, bf16 = jnp.float32, jnp.bfloat16
    vmem = pl.BlockSpec(memory_space=pltpu.VMEM)
    hbm = pl.BlockSpec(memory_space=pltpu.HBM)
    dma = pltpu.SemaphoreType.DMA
    return pl.pallas_call(
        kernel,
        out_shape=pltpu.VMEM((MINE, ROWS, LAGS), f32),
        in_specs=[hbm] * 6,
        out_specs=vmem,
        scratch_shapes=[
            pltpu.SMEM((NSRC,), jnp.int32),
            pltpu.VMEM((1, ROWS), jnp.int32),
            pltpu.VMEM((ROWS, HALF), f32),
            pltpu.VMEM(small.shape, f32),
            pltpu.VMEM(forward.shape, bf16),
            pltpu.VMEM(inverse.shape, bf16),
            pltpu.VMEM((SEGS + 1, ROWS, HALF), f32),
            pltpu.VMEM((SEGS, ROWS, LANES), f32),
            pltpu.VMEM((ROWS, LANES), f32),
            pltpu.VMEM((9, LANES), f32),
            pltpu.VMEM((OWNERS, 9, LANES), f32),
            pltpu.VMEM((9, LANES), f32),
            pltpu.VMEM((SEGS * MINE, 9, LANES), f32),
            pltpu.VMEM((SEGS, 8, ROWS, 256), f32),
            pltpu.VMEM((8, SEGS * MINE, 256), f32),
            dma((6,)), dma((SEGS,)), dma((SEGS,)), dma((SEGS,)), dma((SEGS,)),
            dma((OWNERS,)), dma((OWNERS,)), dma((16,)), dma((16,)), pltpu.SemaphoreType.REGULAR((16,)),
        ],
        compiler_params=pltpu.CompilerParams(
            collective_id=0, has_side_effects=True, vmem_limit_bytes=60 * 2**20
        ),
        name="correlate",
    )(source_channels, valid_mask.reshape(1, ROWS), record, jnp.asarray(small), jnp.asarray(forward), jnp.asarray(inverse))


def solution(mesh):
    placed = (P("recv", "tm"), P(), P("recv", "tm"))
    return jax.shard_map(
        local, mesh=mesh, in_specs=placed, out_specs=P("tm", "recv", None), check_vma=False
    )
```
